32 devices in a mesh: sec: 4 (over y, x), ctx: 2 (over core), ch: 4 (over z).
Axes of the slice: x: 2, y: 2, z: 4, core: 2. Of those that a mesh axis runs over, the one named last changes fastest.
Arguments:
- inputs: bfloat16 [256, 4096], P('ctx', ('ch', 'sec')), may hold values from -2500 to 2500, as said below
- query_fields: bfloat16 [4, 256, 4096], P('sec', 'ctx', 'ch'), may hold values from -3 to 3
- key_fields: bfloat16 [4, 256, 4096], P('sec', 'ctx', 'ch'), may hold values from -4 to 4
- norm_gain: float32 [4096], P('ch'), may hold values from 0.1 to 1.9
- short_taps: float32 [2, 7, 4096], P(None, None, 'ch'), may hold values from -2 to 2
- medium_taps: float32 [128, 4096], P(None, 'ch'), may hold values from -0.5 to 0.5
- pole_rates: float32 [8, 4096], P(None, 'ch'), as said below
- pole_residues: float32 [8, 4096], P(None, 'ch'), may hold values from -2 to 2
- direct_term: float32 [4096], P('ch'), may hold values from -3 to 3
Outputs:
- mixed_stream: bfloat16 [256, 4096], P('ctx', ('ch', 'sec'))
The draws below stay inside these ranges and needn't reach their ends.
Inputs may be any that keep to these rules, and one draw needn't show every extreme that they name: `inputs`: scaled real values. `pole_rates`: Positive, from 0.2 / 256 to 1 / 30.
All inputs are finite; a program needn't handle non-finite values.
Results may differ from the reference program's by a relative error of at most 0.013.
Values may be sent and summed in bfloat16 or wider, within the bound.
A program may use at most 64 MiB of HBM per device.

```python
import math
import jax
import jax.numpy as jnp
from jax import lax

D = 4096
SHORT = 7
MEDIUM = 128
MODES = 8
SECS = 4
TOKENS = 256
N_SEC = 4
N_CH = 4


def draw_inputs(key, part):
    rows_key, rough_key, base_key = jax.random.split(key, 3)
    rises = jnp.arange(D, dtype=jnp.float32) / D
    base_values = jax.random.truncated_normal(base_key, -6.0, 6.0, (TOKENS, D), jnp.float32)
    row_scale = jnp.exp(jax.random.uniform(rows_key, (TOKENS, 1), jnp.float32, 0.0, math.log(10.0)))
    col_scale = jnp.exp(rises * math.log(10.0))
    roughness = jax.random.uniform(rough_key, (D,), jnp.float32, 0.5, 1.5)
    return (base_values * row_scale * (col_scale * roughness)[None]).astype(jnp.bfloat16)


def draw_pole_rates(key, part):
    pick_key, slow_key, fast_key = jax.random.split(key, 3)
    grid_shape = (MODES, D)
    slow_rates = jnp.exp(jax.random.uniform(slow_key, grid_shape, jnp.float32, math.log(0.2), math.log(2.0))) / TOKENS
    fast_rates = jnp.exp(jax.random.uniform(fast_key, grid_shape, jnp.float32, math.log(2.0 / TOKENS), math.log(1.0 / 30.0)))
    slow_share = 0.5
    picked = jax.random.uniform(pick_key, grid_shape, jnp.float32) < slow_share
    return jnp.where(picked, slow_rates, fast_rates).astype(jnp.float32)


def steps_of(own_key, shape, cuts, low, high):
    gain, own = 1.0, jax.random.fold_in(own_key, 6)
    for position, blocks in cuts:
        heights = jnp.exp(jax.random.uniform(jax.random.fold_in(own, position), (blocks,), jnp.float32, low / len(cuts), high / len(cuts)))
        gain = gain * jnp.repeat(heights, shape[position] // blocks).reshape([-1 if axis == position else 1 for axis in range(len(shape))])
    return gain


def centred(own_key, shape, width, bound, cuts=(), held_as=jnp.bfloat16):
    gain = steps_of(own_key, shape, cuts, -0.22, 0.18) if cuts else 1.0
    array = jax.random.normal(own_key, shape, jnp.float32) * width * gain
    return jnp.minimum(jnp.maximum(array, -bound), bound).astype(held_as)


def setup_inputs(seed: int = 0) -> dict:
    streams_of = jax.random.split(jax.random.key(seed), 10)
    return {
        "inputs": draw_inputs(jax.random.fold_in(streams_of[9], 71), 0),
        "query_fields": centred(streams_of[1], (SECS, TOKENS, D), 0.5, 3.0, ((0, 4), (1, 2), (2, 4))),
        "key_fields": centred(streams_of[2], (SECS, TOKENS, D), 1.0, 4.0, ((0, 4), (1, 2), (2, 4))),
        "norm_gain": jnp.clip(1.0 + 0.18 * jax.random.normal(streams_of[3], (D,), jnp.float32), 0.1, 1.9),
        "short_taps": centred(streams_of[4], (2, SHORT, D), SHORT ** -0.5, 2.0, ((2, 4),), jnp.float32),
        "medium_taps": centred(streams_of[5], (MEDIUM, D), MEDIUM ** -0.5, 0.5, ((1, 4),), jnp.float32),
        "pole_rates": draw_pole_rates(jax.random.fold_in(streams_of[9], 71), 0),
        "pole_residues": centred(streams_of[7], (MODES, D), MODES ** -0.5, 2.0, ((1, 4),), jnp.float32),
        "direct_term": centred(streams_of[8], (D,), 0.5, 3.0, ((0, 4),), jnp.float32),
    }


norm_eps = 1e-06

def depthwise(padded, flipped_taps):
    channels = padded.shape[1]
    result = lax.conv_general_dilated(padded[None], flipped_taps[:, None, :], window_strides=(1,), padding='VALID', dimension_numbers=('NWC', 'WIO', 'NWC'), feature_group_count=channels, precision=lax.Precision.HIGHEST)
    return result[0]

def causal_filter(gated, filter_taps):
    span = filter_taps.shape[0]
    padded = jnp.concatenate([jnp.zeros((span - 1, gated.shape[1]), jnp.float32), gated], axis=0)
    return depthwise(padded, jnp.flip(filter_taps, 0))

def modal_recurrence(gated, rates, residues, direct):
    decays = jnp.exp(-rates)
    weights = residues * jnp.sqrt(-jnp.expm1(-2.0 * rates))

    def advance(states, new_row):
        states = decays * states + new_row[None]
        return (states, lax.optimization_barrier(jnp.sum(weights * states, axis=0)))
    initial = jnp.zeros(rates.shape, jnp.float32)
    last_state, outputs = lax.scan(advance, initial, gated)
    return outputs + direct[None] * gated

def reference(inputs, query_fields, key_fields, norm_gain, short_taps, medium_taps, pole_rates, pole_residues, direct_term):
    values = inputs.astype(jnp.float32)
    inverse_rms = lax.rsqrt(lax.optimization_barrier(jnp.mean(values * values, axis=1)) + norm_eps)
    stream = (values * inverse_rms[:, None] * norm_gain[None]).astype(jnp.bfloat16)
    block_width = D // (N_CH * N_SEC)
    block_count = N_CH * N_SEC

    def one_block(block_index):
        offset = block_index * block_width

        def channel_cut(tables):
            return lax.dynamic_slice_in_dim(tables, offset, block_width, tables.ndim - 1)
        current = channel_cut(stream)
        for section in range(4):
            query_block = channel_cut(query_fields[section])
            key_block = channel_cut(key_fields[section])
            gated = key_block.astype(jnp.float32) * current.astype(jnp.float32)
            if section == 0:
                filtered = causal_filter(gated, channel_cut(short_taps[0]))
            elif section == 1:
                filtered = causal_filter(gated, channel_cut(medium_taps))
            elif section == 2:
                filtered = modal_recurrence(gated, channel_cut(pole_rates), channel_cut(pole_residues), channel_cut(direct_term))
            else:
                filtered = causal_filter(gated, channel_cut(short_taps[1]))
            current = (current.astype(jnp.float32) + query_block.astype(jnp.float32) * filtered).astype(jnp.bfloat16)
        return current
    blocks = lax.map(one_block, jnp.arange(block_count, dtype=jnp.int32))
    return jnp.transpose(blocks, (1, 0, 2)).reshape(TOKENS, D)
```

```python
import functools

import jax
import jax.numpy as jnp
from jax import lax
from jax.experimental import pallas as pl
from jax.experimental.pallas import tpu as pltpu
from jax.sharding import PartitionSpec as P

norm_eps = 1e-06
MESH = pl.DeviceIdType.MESH
LANES = 128
ROWS = 8
F32 = jnp.float32


def row_ids(shape):
    return lax.broadcasted_iota(jnp.int32, shape, 0)


def shifted(values, steps):
    if steps == 0:
        return values, jnp.zeros((ROWS, values.shape[1]), F32)
    moved = pltpu.roll(values, steps, 0)
    top = moved[:ROWS]
    inside = row_ids(top.shape) >= steps
    first = jnp.where(inside, top, 0.0)
    if values.shape[0] > ROWS:
        first = jnp.concatenate([first, moved[ROWS:]], axis=0)
    return first, jnp.where(inside, 0.0, top)


def filter_within(values, taps):
    length = values.shape[0]
    span = taps.shape[0]
    total = jnp.zeros(values.shape, F32)
    for step in range(min(ROWS, span)):
        moved, _ = shifted(values, step)
        for tap in range(step, min(span, length), ROWS):
            base = tap - step
            part = moved[: length - base] * taps[tap : tap + 1]
            if base:
                total = jnp.concatenate([total[:base], total[base:] + part], axis=0)
            else:
                total = total + part
    return total


def filter_before(history, taps, length, own=0):
    span = taps.shape[0]
    known = history.shape[0] - own
    total = jnp.zeros((length, history.shape[1]), F32)
    for step in range(min(ROWS, span)):
        moved, fallen = shifted(history, step)
        joined = jnp.concatenate([moved, fallen], axis=0)
        for tap in range(step, span, ROWS):
            base = tap - step
            reach = min(base + ROWS + own, length)
            part = joined[known - base : known - base + reach] * taps[tap : tap + 1]
            if reach < length:
                total = jnp.concatenate([total[:reach] + part, total[reach:]], axis=0)
            else:
                total = total + part
    return total


def kernel(
    sections,
    n_ctx,
    n_ch,
    inputs,
    query,
    key,
    gain,
    short,
    medium,
    rates,
    residues,
    direct,
    out,
    x_ref,
    gain_ref,
    short_ref,
    medium_ref,
    rate_ref,
    residue_ref,
    direct_ref,
    key_ref,
    query_ref,
    sums_sec,
    sums_ch,
    gated_ref,
    filtered_ref,
    stream_ref,
    tail_ref,
    rows_ref,
    state_ref,
    leaving_ref,
    taps_ref,
    age_ref,
    carry_ref,
    top_ref,
    load_sem,
    key_send,
    key_recv,
    query_send,
    query_recv,
    sec_send,
    sec_recv,
    ch_send,
    ch_recv,
    ctx_send,
    ctx_recv,
):
    length, width = x_ref.shape
    modes = rate_ref.shape[0]
    sec = lax.axis_index("sec")
    ctx = lax.axis_index("ctx")
    ch = lax.axis_index("ch")
    has_before = ctx > 0
    has_after = ctx < n_ctx - 1

    def cut(index):
        return pl.ds(pl.multiple_of(index * width, width), width)

    mine = cut(sec)
    loads = [
        pltpu.make_async_copy(inputs, x_ref, load_sem.at[0]),
        pltpu.make_async_copy(rates.at[:, mine], rate_ref, load_sem.at[1]),
        pltpu.make_async_copy(residues.at[:, mine], residue_ref, load_sem.at[2]),
        pltpu.make_async_copy(direct.at[:, mine], direct_ref, load_sem.at[3]),
        pltpu.make_async_copy(gain.at[:, mine], gain_ref, load_sem.at[4]),
        pltpu.make_async_copy(short.at[:, :, mine], short_ref, load_sem.at[5]),
        pltpu.make_async_copy(medium.at[:, mine], medium_ref, load_sem.at[6]),
        pltpu.make_async_copy(key.at[0, :, mine], key_ref.at[sec], key_recv.at[sec]),
        pltpu.make_async_copy(query.at[0, :, mine], query_ref.at[sec], query_recv.at[sec]),
    ]
    for load in loads:
        load.start()

    sec_peers = [lax.rem(sec + step, sections) for step in range(1, sections)]
    ch_peers = [lax.rem(ch + step, n_ch) for step in range(1, n_ch)]
    barrier = pltpu.get_barrier_semaphore()
    for peer in sec_peers:
        pl.semaphore_signal(barrier, inc=1, device_id={"sec": peer}, device_id_type=MESH)
    for peer in ch_peers:
        pl.semaphore_signal(barrier, inc=1, device_id={"ch": peer}, device_id_type=MESH)

    @pl.when(has_before)
    def _():
        pl.semaphore_signal(barrier, inc=1, device_id={"ctx": ctx - 1}, device_id_type=MESH)

    @pl.when(has_after)
    def _():
        pl.semaphore_signal(barrier, inc=1, device_id={"ctx": ctx + 1}, device_id_type=MESH)

    loads[0].wait()
    squares = jnp.square(x_ref[...].astype(F32))
    folded = sum(squares[:, low : low + LANES] for low in range(0, width, LANES))
    partial = jnp.sum(folded.T, axis=0, keepdims=True)
    sums_sec[sec] = partial

    around = has_before.astype(jnp.int32) + has_after.astype(jnp.int32)
    pl.semaphore_wait(barrier, len(sec_peers) + len(ch_peers) + around)

    def remote(src, dst, send_sem, recv_sem, device):
        return pltpu.make_async_remote_copy(
            src_ref=src,
            dst_ref=dst,
            send_sem=send_sem,
            recv_sem=recv_sem,
            device_id=device,
            device_id_type=MESH,
        )

    sends = []
    for step, peer in enumerate(sec_peers):
        slot = sums_sec.at[sec]
        sends.append(remote(slot, slot, sec_send.at[step], sec_recv.at[sec], {"sec": peer}))
    for field, held, send_sem, recv_sem in (
        (key, key_ref, key_send, key_recv),
        (query, query_ref, query_send, query_recv),
    ):
        for step, peer in enumerate(sec_peers):
            sends.append(
                remote(
                    field.at[0, :, cut(peer)],
                    held.at[sec],
                    send_sem.at[step],
                    recv_sem.at[sec],
                    {"sec": peer},
                )
            )
    for send in sends:
        send.start()

    def arrived(ref, sem):
        pltpu.make_async_copy(ref, ref, sem).wait()

    for load in loads[1:4]:
        load.wait()
    offsets = row_ids((length, width)).astype(F32)
    rate_table = rate_ref[...]
    weights = residue_ref[...] * jnp.sqrt(1.0 - jnp.exp(-2.0 * rate_table))
    taps = jnp.where(row_ids((length, width)) == 0, direct_ref[...], 0.0)
    for mode in range(modes):
        part = weights[mode : mode + 1] * jnp.exp(-rate_table[mode : mode + 1] * offsets)
        carry_ref[mode] = part
        taps = taps + part
    taps_ref[...] = taps

    for peer in sec_peers:
        arrived(sums_sec.at[peer], sec_recv.at[peer])
    total = sums_sec[0]
    for index in range(1, sections):
        total = total + sums_sec[index]
    sums_ch[ch] = total
    for step, peer in enumerate(ch_peers):
        slot = sums_ch.at[ch]
        send = remote(slot, slot, ch_send.at[step], ch_recv.at[ch], {"ch": peer})
        send.start()
        sends.append(send)

    @pl.when(has_after)
    def _():
        ages = (length - 1.0) - offsets
        for mode in range(modes):
            age_ref[mode] = jnp.exp(-rate_table[mode : mode + 1] * ages)

    for load in loads[4:7]:
        load.wait()

    for peer in ch_peers:
        arrived(sums_ch.at[peer], ch_recv.at[peer])
    total = sums_ch[0]
    for index in range(1, n_ch):
        total = total + sums_ch[index]
    inverse = lax.rsqrt(total / (width * sections * n_ch) + norm_eps)
    scale = jnp.broadcast_to(inverse[:1], (length, length)).T[:, :1]
    stream = x_ref[...].astype(F32) * scale * gain_ref[...]
    stream_ref[...] = stream.astype(jnp.bfloat16).astype(F32)

    halves = [slice(low, low + LANES) for low in range(0, width, LANES)]
    after = {"ctx": lax.rem(ctx + 1, n_ctx)}

    def short_section(section, tap_set, tail_slot):
        hand = remote(
            gated_ref.at[section, pl.ds(length - ROWS, ROWS)],
            tail_ref.at[tail_slot],
            ctx_send.at[section],
            ctx_recv.at[section],
            after,
        )

        @pl.when(has_after)
        def _():
            hand.start()

        for half in halves:
            filtered_ref[:, half] = filter_within(
                gated_ref[section, :, half], short_ref[:, tap_set, half]
            )

        if section:

            @pl.when(has_before)
            def _():
                hand.wait_recv()
                finish_top(tail_slot, tap_set)

        return hand

    def finish_top(tail_slot, tap_set):
        for half in halves:
            filtered_ref[:ROWS, half] += filter_before(
                tail_ref[tail_slot, :, half], short_ref[:, tap_set, half], ROWS
            )

    def medium_section(section, earlier):
        @pl.when(has_before)
        def _():
            gated_ref[section, :ROWS] = jnp.zeros((ROWS, width), F32)

        hand = remote(
            gated_ref.at[section], rows_ref, ctx_send.at[section], ctx_recv.at[section], after
        )

        @pl.when(jnp.logical_and(has_after, jnp.logical_not(has_before)))
        def _():
            hand.start()

        for half in halves:
            filtered_ref[:, half] = filter_within(
                gated_ref[section, :, half], medium_ref[:, half]
            )

        @pl.when(has_before)
        def _():
            earlier.wait_recv()
            for half in halves:
                added = filter_before(tail_ref[0, :, half], short_ref[:, 0, half], ROWS)
                gate = query_ref[section - 1, :ROWS, half].astype(F32)
                top = top_ref[0, :, half] + gate * (top_ref[1, :, half] + added)
                top = top.astype(jnp.bfloat16).astype(F32)
                stream_ref[:ROWS, half] = top
                gated_ref[section, :ROWS, half] = key_ref[section, :ROWS, half].astype(F32) * top

        @pl.when(jnp.logical_and(has_after, has_before))
        def _():
            hand.start()

        @pl.when(has_before)
        def _():
            hand.wait_recv()
            for half in halves:
                history = jnp.concatenate(
                    [rows_ref[:, half], gated_ref[section, :ROWS, half]], axis=0
                )
                filtered_ref[:, half] += filter_before(
                    history, medium_ref[:, half], length, ROWS
                )

        return hand

    def long_section(section):
        hand = remote(leaving_ref, state_ref, ctx_send.at[section], ctx_recv.at[section], after)

        @pl.when(has_after)
        def _():
            for mode in range(modes):
                leaving_ref[mode : mode + 1] = jnp.sum(
                    age_ref[mode] * gated_ref[section], axis=0, keepdims=True
                )

        @pl.when(jnp.logical_and(has_after, jnp.logical_not(has_before)))
        def _():
            hand.start()

        @pl.when(has_before)
        def _():
            hand.wait_recv()

        @pl.when(jnp.logical_and(has_after, has_before))
        def _():
            leaving_ref[...] += jnp.exp(-length * rate_ref[...]) * state_ref[...]
            hand.start()

        for half in halves:
            filtered_ref[:, half] = filter_within(gated_ref[section, :, half], taps_ref[:, half])

        @pl.when(has_before)
        def _():
            entering = jnp.exp(-rate_ref[...]) * state_ref[...]
            for half in halves:
                carried = filtered_ref[:, half]
                for mode in range(modes):
                    carried = carried + carry_ref[mode, :, half] * entering[mode : mode + 1, half]
                filtered_ref[:, half] = carried

        return hand

    hands = []
    for section in range(sections):
        arrived(key_ref.at[section], key_recv.at[section])
        gated_ref[section] = key_ref[section].astype(F32) * stream_ref[...]
        if section == 1:
            hands.append(medium_section(section, hands[0]))
        elif section == 2:
            hands.append(long_section(section))
        else:
            hands.append(short_section(section, min(section, 1), min(section, 1)))
        arrived(query_ref.at[section], query_recv.at[section])
        if section == 0:
            top_ref[0] = stream_ref[:ROWS]
            top_ref[1] = filtered_ref[:ROWS]
        stream = stream_ref[...] + query_ref[section].astype(F32) * filtered_ref[...]
        if section == sections - 1:
            out[...] = stream.astype(jnp.bfloat16)
        else:
            stream_ref[...] = stream.astype(jnp.bfloat16).astype(F32)

    for send in sends:
        send.wait_send()

    @pl.when(has_after)
    def _():
        for hand in hands:
            hand.wait_send()


def shards(
    inputs,
    query_fields,
    key_fields,
    norm_gain,
    short_taps,
    medium_taps,
    pole_rates,
    pole_residues,
    direct_term,
):
    sections = lax.axis_size("sec")
    n_ctx = lax.axis_size("ctx")
    n_ch = lax.axis_size("ch")
    length, width = inputs.shape
    modes = pole_rates.shape[0]
    shorts, short_span = short_taps.shape[:2]
    hbm = pl.BlockSpec(memory_space=pltpu.HBM)
    anywhere = pl.BlockSpec(memory_space=pl.ANY)
    dma = pltpu.SemaphoreType.DMA
    return pl.pallas_call(
        functools.partial(kernel, sections, n_ctx, n_ch),
        out_shape=jax.ShapeDtypeStruct((length, width), inputs.dtype),
        in_specs=[anywhere] * 9,
        out_specs=pl.BlockSpec(memory_space=pltpu.VMEM),
        scratch_shapes=[
            pltpu.VMEM((length, width), inputs.dtype),
            pltpu.VMEM((1, width), F32),
            pltpu.VMEM((short_span, shorts, width), F32),
            pltpu.VMEM((medium_taps.shape[0], width), F32),
            pltpu.VMEM((modes, width), F32),
            pltpu.VMEM((modes, width), F32),
            pltpu.VMEM((1, width), F32),
            pltpu.VMEM((sections, length, width), key_fields.dtype),
            pltpu.VMEM((sections, length, width), query_fields.dtype),
            pltpu.VMEM((sections, 1, length), F32),
            pltpu.VMEM((n_ch, 1, length), F32),
            pltpu.VMEM((sections, length, width), F32),
            pltpu.VMEM((length, width), F32),
            pltpu.VMEM((length, width), F32),
            pltpu.VMEM((2, ROWS, width), F32),
            pltpu.VMEM((length, width), F32),
            pltpu.VMEM((modes, width), F32),
            pltpu.VMEM((modes, width), F32),
            pltpu.VMEM((length, width), F32),
            pltpu.VMEM((modes, length, width), F32),
            pltpu.VMEM((modes, length, width), F32),
            pltpu.VMEM((2, ROWS, width), F32),
            dma((7,)),
            dma((sections - 1,)),
            dma((sections,)),
            dma((sections - 1,)),
            dma((sections,)),
            dma((sections - 1,)),
            dma((sections,)),
            dma((n_ch - 1,)),
            dma((n_ch,)),
            dma((sections,)),
            dma((sections,)),
        ],
        compiler_params=pltpu.CompilerParams(collective_id=0, has_side_effects=True, vmem_limit_bytes=8*2**20),
    )(*[pltpu.with_memory_space_constraint(a, pltpu.HBM) for a in (
        inputs,
        query_fields,
        key_fields,
        norm_gain[None],
        jnp.swapaxes(short_taps, 0, 1),
        medium_taps,
        pole_rates,
        pole_residues,
        direct_term[None],
    )])


def solution(mesh):
    in_specs = (
        P("ctx", ("ch", "sec")),
        P("sec", "ctx", "ch"),
        P("sec", "ctx", "ch"),
        P("ch"),
        P(None, None, "ch"),
        P(None, "ch"),
        P(None, "ch"),
        P(None, "ch"),
        P("ch"),
    )
    out_specs = P("ctx", ("ch", "sec"))
    return jax.shard_map(shards, mesh=mesh, in_specs=in_specs, out_specs=out_specs, check_vma=False)
```

```python
import functools

import jax
import jax.numpy as jnp
from jax import lax
from jax.experimental import pallas as pl
from jax.experimental.pallas import tpu as pltpu
from jax.sharding import PartitionSpec as P

norm_eps = 1e-06
MESH = pl.DeviceIdType.MESH
LANES = 128
ROWS = 8
F32 = jnp.float32


def row_ids(shape):
    return lax.broadcasted_iota(jnp.int32, shape, 0)


def shifted(values, steps):
    if steps == 0:
        return values, jnp.zeros((ROWS, values.shape[1]), F32)
    moved = pltpu.roll(values, steps, 0)
    top = moved[:ROWS]
    inside = row_ids(top.shape) >= steps
    first = jnp.where(inside, top, 0.0)
    if values.shape[0] > ROWS:
        first = jnp.concatenate([first, moved[ROWS:]], axis=0)
    return first, jnp.where(inside, 0.0, top)


def filter_within(values, taps):
    length = values.shape[0]
    span = taps.shape[0]
    total = jnp.zeros(values.shape, F32)
    for step in range(min(ROWS, span)):
        moved, _ = shifted(values, step)
        for tap in range(step, min(span, length), ROWS):
            base = tap - step
            part = moved[: length - base] * taps[tap : tap + 1]
            if base:
                total = jnp.concatenate([total[:base], total[base:] + part], axis=0)
            else:
                total = total + part
    return total


def filter_before(history, taps, length, own=0):
    span = taps.shape[0]
    known = history.shape[0] - own
    total = jnp.zeros((length, history.shape[1]), F32)
    for step in range(min(ROWS, span)):
        moved, fallen = shifted(history, step)
        joined = jnp.concatenate([moved, fallen], axis=0)
        for tap in range(step, span, ROWS):
            base = tap - step
            reach = min(base + ROWS + own, length)
            part = joined[known - base : known - base + reach] * taps[tap : tap + 1]
            if reach < length:
                total = jnp.concatenate([total[:reach] + part, total[reach:]], axis=0)
            else:
                total = total + part
    return total


def kernel(
    sections,
    n_ctx,
    n_ch,
    inputs,
    query,
    key,
    gain,
    short,
    medium,
    rates,
    residues,
    direct,
    out,
    x_ref,
    gain_ref,
    short_ref,
    medium_ref,
    rate_ref,
    residue_ref,
    direct_ref,
    key_ref,
    query_ref,
    sums_ref,
    gated_ref,
    filtered_ref,
    stream_ref,
    tail_ref,
    rows_ref,
    state_ref,
    leaving_ref,
    taps_ref,
    age_ref,
    carry_ref,
    top_ref,
    load_sem,
    key_send,
    key_recv,
    query_send,
    query_recv,
    sum_send,
    sum_recv,
    ctx_send,
    ctx_recv,
    down_sem,
    ready_sem,
):
    length, width = x_ref.shape
    modes = rate_ref.shape[0]
    sec = lax.axis_index("sec")
    ctx = lax.axis_index("ctx")
    ch = lax.axis_index("ch")
    has_before = ctx > 0
    has_after = ctx < n_ctx - 1

    def cut(index):
        return pl.ds(pl.multiple_of(index * width, width), width)

    mine = cut(sec)
    loads = [
        pltpu.make_async_copy(inputs, x_ref, load_sem.at[0]),
        pltpu.make_async_copy(rates.at[:, mine], rate_ref, load_sem.at[1]),
        pltpu.make_async_copy(residues.at[:, mine], residue_ref, load_sem.at[2]),
        pltpu.make_async_copy(direct.at[:, mine], direct_ref, load_sem.at[3]),
        pltpu.make_async_copy(gain.at[:, mine], gain_ref, load_sem.at[4]),
        pltpu.make_async_copy(short.at[:, :, mine], short_ref, load_sem.at[5]),
        pltpu.make_async_copy(medium.at[:, mine], medium_ref, load_sem.at[6]),
        pltpu.make_async_copy(key.at[0, :, mine], key_ref.at[sec], key_recv.at[sec]),
        pltpu.make_async_copy(query.at[0, :, mine], query_ref.at[sec], query_recv.at[sec]),
    ]
    for load in loads:
        load.start()

    sec_peers = [lax.rem(sec + step, sections) for step in range(1, sections)]
    barrier = pltpu.get_barrier_semaphore()

    def signal(near, sem, device):
        @pl.when(near)
        def _():
            pl.semaphore_signal(sem, inc=1, device_id=device, device_id_type=MESH)

    everyone = [lax.rem(sec + step, sections) for step in range(sections)]

    def planes(ahead):
        for step in range(1, n_ch):
            plane = ch + ahead * step
            yield plane, plane < n_ch if ahead > 0 else plane >= 0

    def signal_planes(sem, ahead):
        for plane, inside in planes(ahead):

            @pl.when(inside)
            def _(plane=plane):
                for peer in everyone:
                    pl.semaphore_signal(
                        sem, inc=1, device_id={"sec": peer, "ch": plane}, device_id_type=MESH
                    )

    for peer in sec_peers:
        pl.semaphore_signal(barrier, inc=1, device_id={"sec": peer}, device_id_type=MESH)
    signal(has_after, barrier, {"ctx": ctx + 1})
    signal_planes(barrier, 1)
    pl.semaphore_wait(barrier, len(sec_peers) + has_before.astype(jnp.int32) + sections * ch)
    signal(has_before, ready_sem, {"ctx": ctx - 1})
    signal_planes(down_sem, -1)

    def remote(src, dst, send_sem, recv_sem, device):
        return pltpu.make_async_remote_copy(
            src_ref=src,
            dst_ref=dst,
            send_sem=send_sem,
            recv_sem=recv_sem,
            device_id=device,
            device_id_type=MESH,
        )

    own = ch * sections + sec

    def sum_copy(to_sec, to_ch):
        slot = sums_ref.at[own]
        place = to_ch * sections + to_sec
        return remote(
            slot, slot, sum_send.at[place], sum_recv.at[own], {"sec": to_sec, "ch": to_ch}
        )

    loads[0].wait()
    squares = jnp.square(x_ref[...].astype(F32))
    folded = sum(squares[:, low : low + LANES] for low in range(0, width, LANES))
    sums_ref[own] = jnp.sum(folded.T, axis=0, keepdims=True)

    sends = [sum_copy(peer, ch) for peer in sec_peers]
    for field, held, send_sem, recv_sem in (
        (key, key_ref, key_send, key_recv),
        (query, query_ref, query_send, query_recv),
    ):
        for step, peer in enumerate(sec_peers):
            sends.append(
                remote(
                    field.at[0, :, cut(peer)],
                    held.at[sec],
                    send_sem.at[step],
                    recv_sem.at[sec],
                    {"sec": peer},
                )
            )
    def send_sums(ahead):
        for plane, inside in planes(ahead):

            @pl.when(inside)
            def _(plane=plane):
                for peer in everyone:
                    sum_copy(peer, plane).start()

    for send in sends[: len(sec_peers)]:
        send.start()
    send_sums(-1)
    for send in sends[len(sec_peers) :]:
        send.start()

    @pl.when(ch < n_ch - 1)
    def _():
        pl.semaphore_wait(down_sem, sections * (n_ch - 1 - ch))

    send_sums(1)

    def arrived(ref, sem):
        pltpu.make_async_copy(ref, ref, sem).wait()

    for load in loads[1:4]:
        load.wait()
    offsets = row_ids((length, width)).astype(F32)
    rate_table = rate_ref[...]
    weights = residue_ref[...] * jnp.sqrt(1.0 - jnp.exp(-2.0 * rate_table))
    taps = jnp.where(row_ids((length, width)) == 0, direct_ref[...], 0.0)
    for mode in range(modes):
        part = weights[mode : mode + 1] * jnp.exp(-rate_table[mode : mode + 1] * offsets)
        carry_ref[mode] = part
        taps = taps + part
    taps_ref[...] = taps

    @pl.when(has_after)
    def _():
        ages = (length - 1.0) - offsets
        for mode in range(modes):
            age_ref[mode] = jnp.exp(-rate_table[mode : mode + 1] * ages)

    for load in loads[4:7]:
        load.wait()

    others = [
        (peer, lax.rem(ch + step, n_ch))
        for step in range(n_ch)
        for peer in (everyone if step else sec_peers)
    ]
    for from_sec, from_ch in others:
        place = from_ch * sections + from_sec
        arrived(sums_ref.at[place], sum_recv.at[place])
    total = sums_ref[0]
    for index in range(1, sections * n_ch):
        total = total + sums_ref[index]
    inverse = lax.rsqrt(total / (width * sections * n_ch) + norm_eps)
    scale = jnp.broadcast_to(inverse[:1], (length, length)).T[:, :1]
    stream = x_ref[...].astype(F32) * scale * gain_ref[...]
    stream_ref[...] = stream.astype(jnp.bfloat16).astype(F32)

    @pl.when(has_after)
    def _():
        pl.semaphore_wait(ready_sem, 1)

    halves = [slice(low, low + LANES) for low in range(0, width, LANES)]
    after = {"ctx": lax.rem(ctx + 1, n_ctx)}

    def short_section(section, tap_set, tail_slot):
        hand = remote(
            gated_ref.at[section, pl.ds(length - ROWS, ROWS)],
            tail_ref.at[tail_slot],
            ctx_send.at[section],
            ctx_recv.at[section],
            after,
        )

        @pl.when(has_after)
        def _():
            hand.start()

        for half in halves:
            filtered_ref[:, half] = filter_within(
                gated_ref[section, :, half], short_ref[:, tap_set, half]
            )

        if section:

            @pl.when(has_before)
            def _():
                hand.wait_recv()
                finish_top(tail_slot, tap_set)

        return hand

    def finish_top(tail_slot, tap_set):
        for half in halves:
            filtered_ref[:ROWS, half] += filter_before(
                tail_ref[tail_slot, :, half], short_ref[:, tap_set, half], ROWS
            )

    def medium_section(section, earlier):
        @pl.when(has_before)
        def _():
            gated_ref[section, :ROWS] = jnp.zeros((ROWS, width), F32)

        hand = remote(
            gated_ref.at[section], rows_ref, ctx_send.at[section], ctx_recv.at[section], after
        )

        @pl.when(jnp.logical_and(has_after, jnp.logical_not(has_before)))
        def _():
            hand.start()

        for half in halves:
            filtered_ref[:, half] = filter_within(
                gated_ref[section, :, half], medium_ref[:, half]
            )

        @pl.when(has_before)
        def _():
            earlier.wait_recv()
            for half in halves:
                added = filter_before(tail_ref[0, :, half], short_ref[:, 0, half], ROWS)
                gate = query_ref[section - 1, :ROWS, half].astype(F32)
                top = top_ref[0, :, half] + gate * (top_ref[1, :, half] + added)
                top = top.astype(jnp.bfloat16).astype(F32)
                stream_ref[:ROWS, half] = top
                gated_ref[section, :ROWS, half] = key_ref[section, :ROWS, half].astype(F32) * top

        @pl.when(jnp.logical_and(has_after, has_before))
        def _():
            hand.start()

        @pl.when(has_before)
        def _():
            hand.wait_recv()
            for half in halves:
                history = jnp.concatenate(
                    [rows_ref[:, half], gated_ref[section, :ROWS, half]], axis=0
                )
                filtered_ref[:, half] += filter_before(
                    history, medium_ref[:, half], length, ROWS
                )

        return hand

    def long_section(section):
        hand = remote(leaving_ref, state_ref, ctx_send.at[section], ctx_recv.at[section], after)

        @pl.when(has_after)
        def _():
            for mode in range(modes):
                leaving_ref[mode : mode + 1] = jnp.sum(
                    age_ref[mode] * gated_ref[section], axis=0, keepdims=True
                )

        @pl.when(jnp.logical_and(has_after, jnp.logical_not(has_before)))
        def _():
            hand.start()

        @pl.when(has_before)
        def _():
            hand.wait_recv()

        @pl.when(jnp.logical_and(has_after, has_before))
        def _():
            leaving_ref[...] += jnp.exp(-length * rate_ref[...]) * state_ref[...]
            hand.start()

        for half in halves:
            filtered_ref[:, half] = filter_within(gated_ref[section, :, half], taps_ref[:, half])

        @pl.when(has_before)
        def _():
            entering = jnp.exp(-rate_ref[...]) * state_ref[...]
            for half in halves:
                carried = filtered_ref[:, half]
                for mode in range(modes):
                    carried = carried + carry_ref[mode, :, half] * entering[mode : mode + 1, half]
                filtered_ref[:, half] = carried

        return hand

    hands = []
    for section in range(sections):
        arrived(key_ref.at[section], key_recv.at[section])
        gated_ref[section] = key_ref[section].astype(F32) * stream_ref[...]
        if section == 1:
            hands.append(medium_section(section, hands[0]))
        elif section == 2:
            hands.append(long_section(section))
        else:
            hands.append(short_section(section, min(section, 1), min(section, 1)))
        arrived(query_ref.at[section], query_recv.at[section])
        if section == 0:
            top_ref[0] = stream_ref[:ROWS]
            top_ref[1] = filtered_ref[:ROWS]
        stream = stream_ref[...] + query_ref[section].astype(F32) * filtered_ref[...]
        if section == sections - 1:
            out[...] = stream.astype(jnp.bfloat16)
        else:
            stream_ref[...] = stream.astype(jnp.bfloat16).astype(F32)

    for send in sends:
        send.wait_send()
    for to_sec, to_ch in others[len(sec_peers) :]:
        sum_copy(to_sec, to_ch).wait_send()

    @pl.when(has_after)
    def _():
        for hand in hands:
            hand.wait_send()


def shards(
    inputs,
    query_fields,
    key_fields,
    norm_gain,
    short_taps,
    medium_taps,
    pole_rates,
    pole_residues,
    direct_term,
):
    sections = lax.axis_size("sec")
    n_ctx = lax.axis_size("ctx")
    n_ch = lax.axis_size("ch")
    length, width = inputs.shape
    modes = pole_rates.shape[0]
    shorts, short_span = short_taps.shape[:2]
    hbm = pl.BlockSpec(memory_space=pltpu.HBM)
    anywhere = pl.BlockSpec(memory_space=pl.ANY)
    dma = pltpu.SemaphoreType.DMA
    return pl.pallas_call(
        functools.partial(kernel, sections, n_ctx, n_ch),
        out_shape=jax.ShapeDtypeStruct((length, width), inputs.dtype),
        in_specs=[anywhere] * 9,
        out_specs=pl.BlockSpec(memory_space=pltpu.VMEM),
        scratch_shapes=[
            pltpu.VMEM((length, width), inputs.dtype),
            pltpu.VMEM((1, width), F32),
            pltpu.VMEM((short_span, shorts, width), F32),
            pltpu.VMEM((medium_taps.shape[0], width), F32),
            pltpu.VMEM((modes, width), F32),
            pltpu.VMEM((modes, width), F32),
            pltpu.VMEM((1, width), F32),
            pltpu.VMEM((sections, length, width), key_fields.dtype),
            pltpu.VMEM((sections, length, width), query_fields.dtype),
            pltpu.VMEM((n_ch * sections, 1, length), F32),
            pltpu.VMEM((sections, length, width), F32),
            pltpu.VMEM((length, width), F32),
            pltpu.VMEM((length, width), F32),
            pltpu.VMEM((2, ROWS, width), F32),
            pltpu.VMEM((length, width), F32),
            pltpu.VMEM((modes, width), F32),
            pltpu.VMEM((modes, width), F32),
            pltpu.VMEM((length, width), F32),
            pltpu.VMEM((modes, length, width), F32),
            pltpu.VMEM((modes, length, width), F32),
            pltpu.VMEM((2, ROWS, width), F32),
            dma((7,)),
            dma((sections - 1,)),
            dma((sections,)),
            dma((sections - 1,)),
            dma((sections,)),
            dma((n_ch * sections,)),
            dma((n_ch * sections,)),
            dma((sections,)),
            dma((sections,)),
            pltpu.SemaphoreType.REGULAR,
            pltpu.SemaphoreType.REGULAR,
        ],
        compiler_params=pltpu.CompilerParams(collective_id=0, has_side_effects=True, vmem_limit_bytes=8*2**20),
    )(*[pltpu.with_memory_space_constraint(a, pltpu.HBM) for a in (
        inputs,
        query_fields,
        key_fields,
        norm_gain[None],
        jnp.swapaxes(short_taps, 0, 1),
        medium_taps,
        pole_rates,
        pole_residues,
        direct_term[None],
    )])


def solution(mesh):
    in_specs = (
        P("ctx", ("ch", "sec")),
        P("sec", "ctx", "ch"),
        P("sec", "ctx", "ch"),
        P("ch"),
        P(None, None, "ch"),
        P(None, "ch"),
        P(None, "ch"),
        P(None, "ch"),
        P("ch"),
    )
    out_specs = P("ctx", ("ch", "sec"))
    return jax.shard_map(shards, mesh=mesh, in_specs=in_specs, out_specs=out_specs, check_vma=False)
```

```python
import functools

import jax
import jax.numpy as jnp
import numpy as np
from jax import lax
from jax.experimental import pallas as pl
from jax.experimental.pallas import tpu as pltpu
from jax.sharding import PartitionSpec as P

norm_eps = 1e-06
MESH = pl.DeviceIdType.MESH
LANES = 128
ROWS = 8
F32 = jnp.float32
BF16 = jnp.bfloat16


def row_ids(shape):
    return lax.broadcasted_iota(jnp.int32, shape, 0)


def parts(values):
    high = values.astype(BF16)
    return high, (values - high.astype(F32)).astype(BF16)


def times(table, values):
    return jnp.dot(table, values.astype(BF16), preferred_element_type=F32)


def times_parts(table, values):
    high, low = parts(values)
    return times(table[0], high) + times(table[0], low) + times(table[1], high)


def waves(length):
    size = 2 * length
    order = np.arange(length)
    turn = 2 * np.pi * np.outer(order, np.arange(size)) / size
    ends = np.cos(np.pi * np.arange(size))
    real, imag = np.cos(turn), -np.sin(turn)
    imag[0] = ends
    back_real, back_imag = 2 * real.T / size, 2 * imag.T / size
    back_real[:, 0] /= 2
    back_imag[:, 0] /= 2
    ahead = np.concatenate([real, imag], axis=0)
    back = np.concatenate([back_real, back_imag], axis=1)[:length]
    own = ahead[:, :length]
    high = own.astype(BF16)
    low = (own - high.astype(np.float64)).astype(BF16)
    return np.stack([high, low]), ahead.astype(BF16), back.astype(BF16)


def kernel(
    sections,
    n_ctx,
    n_ch,
    inputs,
    query,
    key,
    gain,
    short,
    medium,
    rates,
    residues,
    direct,
    own_waves,
    all_waves,
    back_waves,
    out,
    x_ref,
    gain_ref,
    short_ref,
    medium_ref,
    rate_ref,
    residue_ref,
    direct_ref,
    key_ref,
    query_ref,
    sums_ref,
    padded_ref,
    gated_ref,
    rows_ref,
    scaled_ref,
    stream_ref,
    state_ref,
    leaving_ref,
    age_ref,
    carry_ref,
    own_ref,
    all_ref,
    back_ref,
    spectra_ref,
    load_sem,
    key_send,
    key_recv,
    query_send,
    query_recv,
    sum_send,
    sum_recv,
    ctx_send,
    ctx_recv,
    peer_sem,
    far_sem,
    ready_sem,
):
    length, width = x_ref.shape
    modes = rate_ref.shape[0]
    sec = lax.axis_index("sec")
    ctx = lax.axis_index("ctx")
    ch = lax.axis_index("ch")
    has_before = ctx > 0
    has_after = ctx < n_ctx - 1

    def cut(index):
        return pl.ds(pl.multiple_of(index * width, width), width)

    mine = cut(sec)
    halves = [slice(low, low + LANES) for low in range(0, width, LANES)]
    loads = [
        pltpu.make_async_copy(inputs, x_ref, load_sem.at[0]),
        pltpu.make_async_copy(rates.at[:, mine], rate_ref, load_sem.at[1]),
        pltpu.make_async_copy(residues.at[:, mine], residue_ref, load_sem.at[2]),
        pltpu.make_async_copy(direct.at[:, mine], direct_ref, load_sem.at[3]),
        pltpu.make_async_copy(gain.at[:, mine], gain_ref, load_sem.at[4]),
        pltpu.make_async_copy(short.at[:, :, mine], short_ref, load_sem.at[5]),
        pltpu.make_async_copy(medium.at[:, mine], medium_ref, load_sem.at[6]),
        pltpu.make_async_copy(key.at[0, :, mine], key_ref.at[sec], key_recv.at[sec]),
        pltpu.make_async_copy(query.at[0, :, mine], query_ref.at[sec], query_recv.at[sec]),
        pltpu.make_async_copy(own_waves, own_ref, load_sem.at[7]),
        pltpu.make_async_copy(all_waves, all_ref, load_sem.at[8]),
        pltpu.make_async_copy(back_waves, back_ref, load_sem.at[9]),
    ]
    for load in loads:
        load.start()

    own = ch * sections + sec
    places = [(to_sec, to_ch) for to_ch in range(n_ch) for to_sec in range(sections)]

    def order(at_sec, at_ch):
        steps = at_sec % 2 + at_sec // 2 + at_ch
        return steps * len(places) + at_ch * sections + at_sec

    turn = order(sec, ch)
    earlier = [order(*place) < turn for place in places]
    later = [order(*place) > turn for place in places]
    level = [ch == to_ch for _, to_ch in places]

    def count(flags):
        return sum(flag.astype(jnp.int32) for flag in flags)

    def every(flags, act):
        for index, place in enumerate(places):

            @pl.when(flags[index])
            def _(index=index, place=place):
                act(index, *place)

    def signal(sem, device):
        pl.semaphore_signal(sem, inc=1, device_id=device, device_id_type=MESH)

    def await_all(sem, number):
        @pl.when(number > 0)
        def _():
            pl.semaphore_wait(sem, number)

    barrier = pltpu.get_barrier_semaphore()
    every(later, lambda _, *at: signal(barrier, {"sec": at[0], "ch": at[1]}))

    @pl.when(has_after)
    def _():
        signal(barrier, {"ctx": ctx + 1})

    await_all(barrier, count(earlier) + has_before.astype(jnp.int32))

    def greet(index, to_sec, to_ch):
        @pl.when(level[index])
        def _():
            signal(peer_sem.at[sec], {"sec": to_sec, "ch": to_ch})

        @pl.when(jnp.logical_not(level[index]))
        def _():
            signal(far_sem, {"sec": to_sec, "ch": to_ch})

    every(earlier, greet)

    @pl.when(has_before)
    def _():
        signal(ready_sem, {"ctx": ctx - 1})

    def remote(src, dst, send_sem, recv_sem, device):
        return pltpu.make_async_remote_copy(
            src_ref=src,
            dst_ref=dst,
            send_sem=send_sem,
            recv_sem=recv_sem,
            device_id=device,
            device_id_type=MESH,
        )

    def send_sum(index, to_sec, to_ch):
        slot = sums_ref.at[own]
        remote(slot, slot, sum_send, sum_recv, {"sec": to_sec, "ch": to_ch}).start()

    def send_field(tables, to_sec):
        field, held, send_sem, recv_sem = tables
        remote(
            field.at[0, :, cut(to_sec)], held.at[sec], send_sem, recv_sem.at[sec], {"sec": to_sec}
        ).start()

    before = [order(to_sec, ch) < turn for to_sec in range(sections)]
    behind = [order(to_sec, ch) > turn for to_sec in range(sections)]

    def send_fields(flags, tables):
        for to_sec, flag in reversed(list(enumerate(flags))):

            @pl.when(flag)
            def _(to_sec=to_sec):
                send_field(tables, to_sec)

    def both(first, second):
        return [jnp.logical_and(one, two) for one, two in zip(first, second)]

    keys = key, key_ref, key_send, key_recv
    queries = query, query_ref, query_send, query_recv
    far = [jnp.logical_not(flag) for flag in level]
    send_fields(before, keys)

    loads[0].wait()
    squares = jnp.square(x_ref[...].astype(F32))
    folded = sum(squares[:, low : low + LANES] for low in range(0, width, LANES))
    sums_ref[own] = jnp.sum(folded.T, axis=0, keepdims=True)

    every(earlier, send_sum)
    for to_sec in range(sections):

        @pl.when(behind[to_sec])
        def _(to_sec=to_sec):
            pl.semaphore_wait(peer_sem.at[to_sec], 1)
            send_sum(ch * sections + to_sec, to_sec, ch)
            send_field(keys, to_sec)

    send_fields([sec != to_sec for to_sec in range(sections)], queries)

    def arrived(ref, sem):
        pltpu.make_async_copy(ref, ref, sem).wait()

    for load in loads[1:7] + loads[9:]:
        load.wait()
    offsets = row_ids((length, width)).astype(F32)
    ages = (length - 1.0) - offsets
    rate_table = rate_ref[...]
    weights = residue_ref[...] * jnp.sqrt(1.0 - jnp.exp(-2.0 * rate_table))
    taps = jnp.where(row_ids((length, width)) == 0, direct_ref[...], 0.0)
    for mode in range(modes):
        rate = rate_table[mode : mode + 1]
        part = weights[mode : mode + 1] * jnp.exp(-rate * offsets)
        carry_ref[mode] = part
        age_ref[mode] = jnp.exp(-rate * ages)
        taps = taps + part
    first = row_ids((length, width)) == 0
    for index, filter_taps in enumerate((medium_ref[...], taps)):
        spectrum = times_parts(own_ref, filter_taps)
        real, imag = spectrum[:length], spectrum[length:]
        spectra_ref[index, 0] = real
        spectra_ref[index, 1] = jnp.where(first, 0.0, imag)
        spectra_ref[index, 2] = jnp.where(first, imag, real)

    scaled_ref[...] = x_ref[...].astype(F32) * gain_ref[...]

    @pl.when(jnp.logical_not(has_before))
    def _():
        padded_ref[:, :, :ROWS] = jnp.zeros((2, len(halves), ROWS, LANES), F32)

    await_all(far_sem, count(both(later, far)))
    every(both(later, far), send_sum)

    peers = len(places) - 1
    arrived(sums_ref.at[pl.ds(0, peers)], sum_recv)
    total = sums_ref[0]
    for index in range(1, len(places)):
        total = total + sums_ref[index]
    inverse = lax.rsqrt(total / (width * len(places)) + norm_eps)
    scale = jnp.broadcast_to(inverse, (length, length)).T
    for half in halves:
        stream_ref[:, half] = scaled_ref[:, half] * scale

    @pl.when(has_after)
    def _():
        pl.semaphore_wait(ready_sem, 1)

    after = {"ctx": lax.rem(ctx + 1, n_ctx)}

    def hand_over(section, src, dst):
        return remote(src, dst, ctx_send.at[section], ctx_recv.at[section], after)

    def gated(section):
        return key_ref[section].astype(F32) * stream_ref[...]

    def advance(section, filtered):
        arrived(query_ref.at[section], query_recv.at[section])
        return stream_ref[...] + query_ref[section].astype(F32) * filtered

    def short_section(section, tap_set):
        hand = hand_over(
            section,
            padded_ref.at[tap_set, :, pl.ds(length, ROWS)],
            padded_ref.at[tap_set, :, pl.ds(0, ROWS)],
        )
        values = gated(section)
        for index, half in enumerate(halves):
            padded_ref[tap_set, index, ROWS:] = values[:, half]

        @pl.when(has_after)
        def _():
            hand.start()

        @pl.when(has_before)
        def _():
            hand.wait_recv()

        filtered = []
        for index, half in enumerate(halves):
            taps = short_ref[:, tap_set, half]
            total = values[:, half] * taps[:1]
            for tap in range(1, taps.shape[0]):
                rows = padded_ref[tap_set, index, pl.ds(ROWS - tap, length)]
                total = total + rows * taps[tap : tap + 1]
            filtered.append(total)
        return hand, advance(section, jnp.concatenate(filtered, axis=1))

    def from_spectrum(index, spectrum):
        real, imag = spectrum[:length], spectrum[length:]
        first, cross, last = (spectra_ref[index, place] for place in range(3))
        product = jnp.concatenate(
            [real * first - imag * cross, real * cross + imag * last], axis=0
        )
        return times(back_ref[...], product)

    def medium_section(section):
        hand = hand_over(section, gated_ref, rows_ref)
        gated_ref[...] = gated(section).astype(BF16)

        @pl.when(has_after)
        def _():
            hand.start()

        arrived(query_ref.at[section], query_recv.at[section])

        def finish(spectrum):
            filtered = from_spectrum(0, spectrum)
            stream_ref[...] += query_ref[section].astype(F32) * filtered

        @pl.when(jnp.logical_not(has_before))
        def _():
            finish(times(own_ref[0], gated_ref[...]))

        @pl.when(has_before)
        def _():
            hand.wait_recv()
            both = jnp.concatenate([gated_ref[...], rows_ref[...]], axis=0)
            finish(times(all_ref[...], both))

        return hand

    def long_section(section):
        hand = hand_over(section, leaving_ref, state_ref)
        values = gated(section)
        arrived(query_ref.at[section], query_recv.at[section])

        def leave():
            for mode in range(modes):
                leaving_ref[mode : mode + 1] = jnp.sum(
                    age_ref[mode] * values, axis=0, keepdims=True
                )

        @pl.when(jnp.logical_not(has_before))
        def _():
            spectrum = times(own_ref[0], values)
            if n_ctx > 1:
                leave()
                hand.start()
            filtered = from_spectrum(1, spectrum)
            stream_ref[...] += query_ref[section].astype(F32) * filtered

        @pl.when(has_before)
        def _():
            spectrum = times(own_ref[0], values)

            @pl.when(has_after)
            def _():
                leave()

            hand.wait_recv()

            @pl.when(has_after)
            def _():
                leaving_ref[...] += jnp.exp(-length * rate_ref[...]) * state_ref[...]
                hand.start()

            entering = jnp.exp(-rate_ref[...]) * state_ref[...]
            filtered = from_spectrum(1, spectrum)
            for mode in range(modes):
                filtered = filtered + carry_ref[mode] * entering[mode : mode + 1]
            stream_ref[...] += query_ref[section].astype(F32) * filtered

        return hand

    hands = []
    for section in range(sections):
        arrived(key_ref.at[section], key_recv.at[section])
        if section == 1:
            hands.append(medium_section(section))
        elif section == 2:
            hands.append(long_section(section))
        else:
            hand, stream = short_section(section, min(section, 1))
            hands.append(hand)
            if section:
                out[...] = stream.astype(BF16)
            else:
                stream_ref[...] = stream

    arrived(sums_ref.at[pl.ds(0, peers)], sum_send)
    arrived(key_ref.at[pl.ds(0, sections - 1)], key_send)
    arrived(query_ref.at[pl.ds(0, sections - 1)], query_send)

    @pl.when(has_after)
    def _():
        for hand in hands:
            hand.wait_send()


def shards(
    inputs,
    query_fields,
    key_fields,
    norm_gain,
    short_taps,
    medium_taps,
    pole_rates,
    pole_residues,
    direct_term,
):
    sections = lax.axis_size("sec")
    n_ctx = lax.axis_size("ctx")
    n_ch = lax.axis_size("ch")
    length, width = inputs.shape
    modes = pole_rates.shape[0]
    shorts, short_span = short_taps.shape[:2]
    tables = waves(length)
    anywhere = pl.BlockSpec(memory_space=pl.ANY)
    dma = pltpu.SemaphoreType.DMA
    return pl.pallas_call(
        functools.partial(kernel, sections, n_ctx, n_ch),
        out_shape=jax.ShapeDtypeStruct((length, width), inputs.dtype),
        in_specs=[anywhere] * 12,
        out_specs=pl.BlockSpec(memory_space=pltpu.VMEM),
        scratch_shapes=[
            pltpu.VMEM((length, width), inputs.dtype),
            pltpu.VMEM((1, width), F32),
            pltpu.VMEM((short_span, shorts, width), F32),
            pltpu.VMEM((medium_taps.shape[0], width), F32),
            pltpu.VMEM((modes, width), F32),
            pltpu.VMEM((modes, width), F32),
            pltpu.VMEM((1, width), F32),
            pltpu.VMEM((sections, length, width), key_fields.dtype),
            pltpu.VMEM((sections, length, width), query_fields.dtype),
            pltpu.VMEM((n_ch * sections, 1, length), F32),
            pltpu.VMEM((2, width // LANES, ROWS + length, LANES), F32),
            pltpu.VMEM((length, width), BF16),
            pltpu.VMEM((length, width), BF16),
            pltpu.VMEM((length, width), F32),
            pltpu.VMEM((length, width), F32),
            pltpu.VMEM((modes, width), F32),
            pltpu.VMEM((modes, width), F32),
            pltpu.VMEM((modes, length, width), F32),
            pltpu.VMEM((modes, length, width), F32),
            pltpu.VMEM(tables[0].shape, BF16),
            pltpu.VMEM(tables[1].shape, BF16),
            pltpu.VMEM(tables[2].shape, BF16),
            pltpu.VMEM((2, 3, length, width), F32),
            dma((10,)),
            dma,
            dma((sections,)),
            dma,
            dma((sections,)),
            dma,
            dma,
            dma((sections,)),
            dma((sections,)),
            pltpu.SemaphoreType.REGULAR((sections,)),
            pltpu.SemaphoreType.REGULAR,
            pltpu.SemaphoreType.REGULAR,
        ],
        compiler_params=pltpu.CompilerParams(collective_id=0, has_side_effects=True, vmem_limit_bytes=8*2**20),
    )(*[pltpu.with_memory_space_constraint(a, pltpu.HBM) for a in (
        inputs,
        query_fields,
        key_fields,
        norm_gain[None],
        jnp.swapaxes(short_taps, 0, 1),
        medium_taps,
        pole_rates,
        pole_residues,
        direct_term[None],
        *(jnp.asarray(table) for table in tables),
    )])


def solution(mesh):
    in_specs = (
        P("ctx", ("ch", "sec")),
        P("sec", "ctx", "ch"),
        P("sec", "ctx", "ch"),
        P("ch"),
        P(None, None, "ch"),
        P(None, "ch"),
        P(None, "ch"),
        P(None, "ch"),
        P("ch"),
    )
    out_specs = P("ctx", ("ch", "sec"))
    return jax.shard_map(shards, mesh=mesh, in_specs=in_specs, out_specs=out_specs, check_vma=False)
```

```python
import functools

import jax
import jax.numpy as jnp
import numpy as np
from jax import lax
from jax.experimental import pallas as pl
from jax.experimental.pallas import tpu as pltpu
from jax.sharding import PartitionSpec as P

norm_eps = 1e-06
MESH = pl.DeviceIdType.MESH
LANES = 128
ROWS = 8
F32 = jnp.float32
BF16 = jnp.bfloat16


def row_ids(shape):
    return lax.broadcasted_iota(jnp.int32, shape, 0)


def parts(values):
    high = values.astype(BF16)
    return high, (values - high.astype(F32)).astype(BF16)


def times(table, values):
    return jnp.dot(table, values.astype(BF16), preferred_element_type=F32)


def times_parts(table, values):
    high, low = parts(values)
    return times(table[0], high) + times(table[0], low) + times(table[1], high)


def waves(length):
    size = 2 * length
    order = np.arange(length)
    turn = 2 * np.pi * np.outer(order, np.arange(size)) / size
    ends = np.cos(np.pi * np.arange(size))
    real, imag = np.cos(turn), -np.sin(turn)
    imag[0] = ends
    back_real, back_imag = 2 * real.T / size, 2 * imag.T / size
    back_real[:, 0] /= 2
    back_imag[:, 0] /= 2
    ahead = np.concatenate([real, imag], axis=0)
    back = np.concatenate([back_real, back_imag], axis=1)[:length]
    own = ahead[:, :length]
    high = own.astype(BF16)
    low = (own - high.astype(np.float64)).astype(BF16)
    return np.stack([high, low]), ahead.astype(BF16), back.astype(BF16)


def kernel(
    sections,
    n_ctx,
    n_ch,
    inputs,
    query,
    key,
    gain,
    short,
    medium,
    rates,
    residues,
    direct,
    own_waves,
    all_waves,
    back_waves,
    out,
    x_ref,
    gain_ref,
    short_ref,
    medium_ref,
    rate_ref,
    residue_ref,
    direct_ref,
    key_ref,
    query_ref,
    sums_ref,
    padded_ref,
    gated_ref,
    rows_ref,
    scaled_ref,
    stream_ref,
    state_ref,
    leaving_ref,
    age_ref,
    carry_ref,
    own_ref,
    all_ref,
    back_ref,
    spectra_ref,
    load_sem,
    key_send,
    key_recv,
    query_send,
    query_recv,
    sum_send,
    sum_recv,
    ctx_send,
    ctx_recv,
    peer_sem,
    far_sem,
    ready_sem,
):
    length, width = x_ref.shape
    modes = rate_ref.shape[0]
    sec = lax.axis_index("sec")
    ctx = lax.axis_index("ctx")
    ch = lax.axis_index("ch")
    has_before = ctx > 0
    has_after = ctx < n_ctx - 1

    def cut(index):
        return pl.ds(pl.multiple_of(index * width, width), width)

    mine = cut(sec)
    halves = [slice(low, low + LANES) for low in range(0, width, LANES)]
    loads = [
        pltpu.make_async_copy(inputs, x_ref, load_sem.at[0]),
        pltpu.make_async_copy(rates.at[:, mine], rate_ref, load_sem.at[1]),
        pltpu.make_async_copy(residues.at[:, mine], residue_ref, load_sem.at[2]),
        pltpu.make_async_copy(direct.at[:, mine], direct_ref, load_sem.at[3]),
        pltpu.make_async_copy(gain.at[:, mine], gain_ref, load_sem.at[4]),
        pltpu.make_async_copy(short.at[:, :, mine], short_ref, load_sem.at[5]),
        pltpu.make_async_copy(medium.at[:, mine], medium_ref, load_sem.at[6]),
        pltpu.make_async_copy(key.at[0, :, mine], key_ref.at[sec], key_recv.at[sec]),
        pltpu.make_async_copy(query.at[0, :, mine], query_ref.at[sec], query_recv.at[sec]),
        pltpu.make_async_copy(own_waves, own_ref, load_sem.at[7]),
        pltpu.make_async_copy(all_waves, all_ref, load_sem.at[8]),
        pltpu.make_async_copy(back_waves, back_ref, load_sem.at[9]),
    ]
    for load in loads:
        load.start()

    own = ch * sections + sec
    members = range(sections)
    places = [(to_sec, to_ch) for to_ch in range(n_ch) for to_sec in members]
    last, top = sections - 1, n_ch - 1
    opens, closes = sec == 0, sec == last
    middle = jnp.logical_not(jnp.logical_or(opens, closes))
    corner = jnp.logical_and(closes, ch == top)

    def also(one, two):
        return jnp.logical_and(one, two)

    def signal(flag, sem, device):
        @pl.when(flag)
        def _():
            pl.semaphore_signal(sem, inc=1, device_id=device, device_id_type=MESH)

    barrier = pltpu.get_barrier_semaphore()
    signal(middle, barrier, {"sec": last})
    for to_sec in members[1:]:
        signal(opens, barrier, {"sec": to_sec})
    signal(ch < top, barrier, {"sec": last, "ch": top})
    signal(has_after, barrier, {"ctx": ctx + 1})
    heard = (
        middle.astype(jnp.int32)
        + closes.astype(jnp.int32) * last
        + corner.astype(jnp.int32) * (sections * top)
        + has_before.astype(jnp.int32)
    )

    @pl.when(heard > 0)
    def _():
        pl.semaphore_wait(barrier, heard)

    for to_sec in members[:-1]:
        signal(closes, peer_sem.at[last], {"sec": to_sec})
    signal(middle, peer_sem.at[sec], {"sec": 0})
    for to_sec, to_ch in places[:-1]:
        signal(corner, far_sem, {"sec": to_sec, "ch": to_ch})
    signal(has_before, ready_sem, {"ctx": ctx - 1})

    def remote(src, dst, send_sem, recv_sem, device):
        return pltpu.make_async_remote_copy(
            src_ref=src,
            dst_ref=dst,
            send_sem=send_sem,
            recv_sem=recv_sem,
            device_id=device,
            device_id_type=MESH,
        )

    def send_sum(to_sec, to_ch):
        slot = sums_ref.at[own]
        remote(slot, slot, sum_send, sum_recv, {"sec": to_sec, "ch": to_ch}).start()

    def send_field(tables, to_sec):
        field, held, send_sem, recv_sem = tables
        remote(
            field.at[0, :, cut(to_sec)], held.at[sec], send_sem, recv_sem.at[sec], {"sec": to_sec}
        ).start()

    def send_far():
        for to_sec, to_ch in places:

            @pl.when(ch != to_ch)
            def _(to_sec=to_sec, to_ch=to_ch):
                send_sum(to_sec, to_ch)

    def each(flag, chosen, act):
        @pl.when(flag)
        def _():
            for to_sec in chosen:
                act(to_sec)

    keys = key, key_ref, key_send, key_recv
    queries = query, query_ref, query_send, query_recv
    each(middle, members[:1], lambda to_sec: send_field(keys, to_sec))
    each(closes, members[:-1], lambda to_sec: send_field(keys, to_sec))

    loads[0].wait()
    squares = jnp.square(x_ref[...].astype(F32))
    folded = sum(squares[:, low : low + LANES] for low in range(0, width, LANES))
    sums_ref[own] = jnp.sum(folded.T, axis=0, keepdims=True)

    pl.when(corner)(send_far)
    each(middle, members[:1], lambda to_sec: send_sum(to_sec, ch))
    each(closes, members[:-1], lambda to_sec: send_sum(to_sec, ch))

    def meet(to_sec):
        pl.semaphore_wait(peer_sem.at[to_sec], 1)
        send_sum(to_sec, ch)
        send_field(keys, to_sec)

    each(opens, members[1:], meet)

    @pl.when(middle)
    def _():
        pl.semaphore_wait(peer_sem.at[last], 1)

    for act in (lambda to_sec: send_sum(to_sec, ch), lambda to_sec: send_field(keys, to_sec)):
        for to_sec in members[1:]:
            each(also(middle, sec != to_sec), [to_sec], act)
    for to_sec in members:
        each(sec != to_sec, [to_sec], lambda to_sec: send_field(queries, to_sec))

    def far_sums():
        pl.semaphore_wait(far_sem, 1)
        send_far()

    steps = sec % 2 + sec // 2 + ch
    late = 2 * steps > last % 2 + last // 2 + top
    pl.when(also(late, jnp.logical_not(corner)))(far_sums)

    def arrived(ref, sem):
        pltpu.make_async_copy(ref, ref, sem).wait()

    for load in loads[1:7] + loads[9:]:
        load.wait()
    offsets = row_ids((length, width)).astype(F32)
    ages = (length - 1.0) - offsets
    rate_table = rate_ref[...]
    weights = residue_ref[...] * jnp.sqrt(1.0 - jnp.exp(-2.0 * rate_table))
    taps = jnp.where(row_ids((length, width)) == 0, direct_ref[...], 0.0)
    for mode in range(modes):
        rate = rate_table[mode : mode + 1]
        part = weights[mode : mode + 1] * jnp.exp(-rate * offsets)
        carry_ref[mode] = part
        age_ref[mode] = jnp.exp(-rate * ages)
        taps = taps + part
    first = row_ids((length, width)) == 0
    for index, filter_taps in enumerate((medium_ref[...], taps)):
        spectrum = times_parts(own_ref, filter_taps)
        real, imag = spectrum[:length], spectrum[length:]
        spectra_ref[index, 0] = real
        spectra_ref[index, 1] = jnp.where(first, 0.0, imag)
        spectra_ref[index, 2] = jnp.where(first, imag, real)

    scaled_ref[...] = x_ref[...].astype(F32) * gain_ref[...]

    @pl.when(jnp.logical_not(has_before))
    def _():
        padded_ref[:, :, :ROWS] = jnp.zeros((2, len(halves), ROWS, LANES), F32)

    pl.when(jnp.logical_not(late))(far_sums)

    peers = len(places) - 1
    arrived(sums_ref.at[pl.ds(0, peers)], sum_recv)
    total = sums_ref[0]
    for index in range(1, len(places)):
        total = total + sums_ref[index]
    inverse = lax.rsqrt(total / (width * len(places)) + norm_eps)
    scale = jnp.broadcast_to(inverse, (length, length)).T
    for half in halves:
        stream_ref[:, half] = scaled_ref[:, half] * scale

    @pl.when(has_after)
    def _():
        pl.semaphore_wait(ready_sem, 1)

    after = {"ctx": lax.rem(ctx + 1, n_ctx)}

    def hand_over(section, src, dst):
        return remote(src, dst, ctx_send.at[section], ctx_recv.at[section], after)

    def gated(section):
        return key_ref[section].astype(F32) * stream_ref[...]

    def advance(section, filtered):
        arrived(query_ref.at[section], query_recv.at[section])
        return stream_ref[...] + query_ref[section].astype(F32) * filtered

    def short_section(section, tap_set):
        hand = hand_over(
            section,
            padded_ref.at[tap_set, :, pl.ds(length, ROWS)],
            padded_ref.at[tap_set, :, pl.ds(0, ROWS)],
        )
        values = gated(section)
        for index, half in enumerate(halves):
            padded_ref[tap_set, index, ROWS:] = values[:, half]

        @pl.when(has_after)
        def _():
            hand.start()

        @pl.when(has_before)
        def _():
            hand.wait_recv()

        filtered = []
        for index, half in enumerate(halves):
            taps = short_ref[:, tap_set, half]
            total = values[:, half] * taps[:1]
            for tap in range(1, taps.shape[0]):
                rows = padded_ref[tap_set, index, pl.ds(ROWS - tap, length)]
                total = total + rows * taps[tap : tap + 1]
            filtered.append(total)
        return hand, advance(section, jnp.concatenate(filtered, axis=1))

    def from_spectrum(index, spectrum):
        real, imag = spectrum[:length], spectrum[length:]
        first, cross, last = (spectra_ref[index, place] for place in range(3))
        product = jnp.concatenate(
            [real * first - imag * cross, real * cross + imag * last], axis=0
        )
        return times(back_ref[...], product)

    def medium_section(section):
        hand = hand_over(section, gated_ref, rows_ref)
        gated_ref[...] = gated(section).astype(BF16)

        @pl.when(has_after)
        def _():
            hand.start()

        arrived(query_ref.at[section], query_recv.at[section])

        def finish(spectrum):
            filtered = from_spectrum(0, spectrum)
            stream_ref[...] += query_ref[section].astype(F32) * filtered

        @pl.when(jnp.logical_not(has_before))
        def _():
            finish(times(own_ref[0], gated_ref[...]))

        @pl.when(has_before)
        def _():
            hand.wait_recv()
            both = jnp.concatenate([gated_ref[...], rows_ref[...]], axis=0)
            finish(times(all_ref[...], both))

        return hand

    def long_section(section):
        hand = hand_over(section, leaving_ref, state_ref)
        values = gated(section)
        arrived(query_ref.at[section], query_recv.at[section])

        def leave():
            for mode in range(modes):
                leaving_ref[mode : mode + 1] = jnp.sum(
                    age_ref[mode] * values, axis=0, keepdims=True
                )

        @pl.when(jnp.logical_not(has_before))
        def _():
            spectrum = times(own_ref[0], values)
            if n_ctx > 1:
                leave()
                hand.start()
            filtered = from_spectrum(1, spectrum)
            stream_ref[...] += query_ref[section].astype(F32) * filtered

        @pl.when(has_before)
        def _():
            spectrum = times(own_ref[0], values)

            @pl.when(has_after)
            def _():
                leave()

            hand.wait_recv()

            @pl.when(has_after)
            def _():
                leaving_ref[...] += jnp.exp(-length * rate_ref[...]) * state_ref[...]
                hand.start()

            entering = jnp.exp(-rate_ref[...]) * state_ref[...]
            filtered = from_spectrum(1, spectrum)
            for mode in range(modes):
                filtered = filtered + carry_ref[mode] * entering[mode : mode + 1]
            stream_ref[...] += query_ref[section].astype(F32) * filtered

        return hand

    hands = []
    for section in range(sections):
        arrived(key_ref.at[section], key_recv.at[section])
        if section == 1:
            hands.append(medium_section(section))
        elif section == 2:
            hands.append(long_section(section))
        else:
            hand, stream = short_section(section, min(section, 1))
            hands.append(hand)
            if section:
                out[...] = stream.astype(BF16)
            else:
                stream_ref[...] = stream

    arrived(sums_ref.at[pl.ds(0, peers)], sum_send)
    arrived(key_ref.at[pl.ds(0, sections - 1)], key_send)
    arrived(query_ref.at[pl.ds(0, sections - 1)], query_send)

    @pl.when(has_after)
    def _():
        for hand in hands:
            hand.wait_send()


def shards(
    inputs,
    query_fields,
    key_fields,
    norm_gain,
    short_taps,
    medium_taps,
    pole_rates,
    pole_residues,
    direct_term,
):
    sections = lax.axis_size("sec")
    n_ctx = lax.axis_size("ctx")
    n_ch = lax.axis_size("ch")
    length, width = inputs.shape
    modes = pole_rates.shape[0]
    shorts, short_span = short_taps.shape[:2]
    tables = waves(length)
    anywhere = pl.BlockSpec(memory_space=pl.ANY)
    dma = pltpu.SemaphoreType.DMA
    return pl.pallas_call(
        functools.partial(kernel, sections, n_ctx, n_ch),
        out_shape=jax.ShapeDtypeStruct((length, width), inputs.dtype),
        in_specs=[anywhere] * 12,
        out_specs=pl.BlockSpec(memory_space=pltpu.VMEM),
        scratch_shapes=[
            pltpu.VMEM((length, width), inputs.dtype),
            pltpu.VMEM((1, width), F32),
            pltpu.VMEM((short_span, shorts, width), F32),
            pltpu.VMEM((medium_taps.shape[0], width), F32),
            pltpu.VMEM((modes, width), F32),
            pltpu.VMEM((modes, width), F32),
            pltpu.VMEM((1, width), F32),
            pltpu.VMEM((sections, length, width), key_fields.dtype),
            pltpu.VMEM((sections, length, width), query_fields.dtype),
            pltpu.VMEM((n_ch * sections, 1, length), F32),
            pltpu.VMEM((2, width // LANES, ROWS + length, LANES), F32),
            pltpu.VMEM((length, width), BF16),
            pltpu.VMEM((length, width), BF16),
            pltpu.VMEM((length, width), F32),
            pltpu.VMEM((length, width), F32),
            pltpu.VMEM((modes, width), F32),
            pltpu.VMEM((modes, width), F32),
            pltpu.VMEM((modes, length, width), F32),
            pltpu.VMEM((modes, length, width), F32),
            pltpu.VMEM(tables[0].shape, BF16),
            pltpu.VMEM(tables[1].shape, BF16),
            pltpu.VMEM(tables[2].shape, BF16),
            pltpu.VMEM((2, 3, length, width), F32),
            dma((10,)),
            dma,
            dma((sections,)),
            dma,
            dma((sections,)),
            dma,
            dma,
            dma((sections,)),
            dma((sections,)),
            pltpu.SemaphoreType.REGULAR((sections,)),
            pltpu.SemaphoreType.REGULAR,
            pltpu.SemaphoreType.REGULAR,
        ],
        compiler_params=pltpu.CompilerParams(collective_id=0, has_side_effects=True, vmem_limit_bytes=8*2**20),
    )(*[pltpu.with_memory_space_constraint(a, pltpu.HBM) for a in (
        inputs,
        query_fields,
        key_fields,
        norm_gain[None],
        jnp.swapaxes(short_taps, 0, 1),
        medium_taps,
        pole_rates,
        pole_residues,
        direct_term[None],
        *(jnp.asarray(table) for table in tables),
    )])


def solution(mesh):
    in_specs = (
        P("ctx", ("ch", "sec")),
        P("sec", "ctx", "ch"),
        P("sec", "ctx", "ch"),
        P("ch"),
        P(None, None, "ch"),
        P(None, "ch"),
        P(None, "ch"),
        P(None, "ch"),
        P("ch"),
    )
    out_specs = P("ctx", ("ch", "sec"))
    return jax.shard_map(shards, mesh=mesh, in_specs=in_specs, out_specs=out_specs, check_vma=False)
```

```python
import functools

import jax
import jax.numpy as jnp
import numpy as np
from jax import lax
from jax.experimental import pallas as pl
from jax.experimental.pallas import tpu as pltpu
from jax.sharding import PartitionSpec as P

norm_eps = 1e-06
MESH = pl.DeviceIdType.MESH
LANES = 128
ROWS = 8
F32 = jnp.float32
BF16 = jnp.bfloat16


def row_ids(shape):
    return lax.broadcasted_iota(jnp.int32, shape, 0)


def parts(values):
    high = values.astype(BF16)
    return high, (values - high.astype(F32)).astype(BF16)


def times(table, values):
    values = values.astype(BF16)
    half = table.shape[0] // 2
    return jnp.concatenate(
        [
            jnp.dot(rows, values, preferred_element_type=F32)
            for rows in (table[:half], table[half:])
        ],
        axis=0,
    )


def times_parts(table, values):
    high, low = parts(values)
    return times(table[0], high) + times(table[0], low) + times(table[1], high)


def waves(length):
    size = 2 * length
    order = np.arange(length)
    turn = 2 * np.pi * np.outer(order, np.arange(size)) / size
    ends = np.cos(np.pi * np.arange(size))
    real, imag = np.cos(turn), -np.sin(turn)
    imag[0] = ends
    back_real, back_imag = 2 * real.T / size, 2 * imag.T / size
    back_real[:, 0] /= 2
    back_imag[:, 0] /= 2
    ahead = np.concatenate([real, imag], axis=0)
    back = np.concatenate([back_real, back_imag], axis=1)[:length]
    own = ahead[:, :length]
    high = own.astype(BF16)
    low = (own - high.astype(np.float64)).astype(BF16)
    return np.stack([high, low]), ahead.astype(BF16), back.astype(BF16)


def kernel(
    sections,
    n_ctx,
    n_ch,
    inputs,
    query,
    key,
    gain,
    short,
    medium,
    rates,
    residues,
    direct,
    own_waves,
    all_waves,
    back_waves,
    out,
    x_ref,
    gain_ref,
    short_ref,
    medium_ref,
    rate_ref,
    residue_ref,
    direct_ref,
    key_ref,
    query_ref,
    sums_ref,
    padded_ref,
    gated_ref,
    rows_ref,
    scaled_ref,
    stream_ref,
    waiting_ref,
    state_ref,
    leaving_ref,
    age_ref,
    carry_ref,
    decay_ref,
    ending_ref,
    within_ref,
    own_ref,
    all_ref,
    back_ref,
    spectra_ref,
    load_sem,
    key_send,
    key_recv,
    query_send,
    query_recv,
    sum_send,
    sum_recv,
    ctx_send,
    ctx_recv,
    peer_sem,
    far_sem,
    ready_sem,
    turn_sem,
):
    length, width = x_ref.shape
    modes = rate_ref.shape[0]
    sec = lax.axis_index("sec")
    ctx = lax.axis_index("ctx")
    ch = lax.axis_index("ch")
    has_before = ctx > 0
    has_after = ctx < n_ctx - 1

    def cut(index):
        return pl.ds(pl.multiple_of(index * width, width), width)

    mine = cut(sec)
    halves = [slice(low, low + LANES) for low in range(0, width, LANES)]
    loads = [
        pltpu.make_async_copy(inputs, x_ref, load_sem.at[0]),
        pltpu.make_async_copy(rates.at[:, mine], rate_ref, load_sem.at[1]),
        pltpu.make_async_copy(residues.at[:, mine], residue_ref, load_sem.at[2]),
        pltpu.make_async_copy(direct.at[:, mine], direct_ref, load_sem.at[3]),
        pltpu.make_async_copy(gain.at[:, mine], gain_ref, load_sem.at[4]),
        pltpu.make_async_copy(short.at[:, :, mine], short_ref, load_sem.at[5]),
        pltpu.make_async_copy(medium.at[:, mine], medium_ref, load_sem.at[6]),
        pltpu.make_async_copy(key.at[0, :, mine], key_ref.at[sec], key_recv.at[sec]),
        pltpu.make_async_copy(query.at[0, :, mine], query_ref.at[sec], query_recv.at[sec]),
        pltpu.make_async_copy(own_waves, own_ref, load_sem.at[7]),
        pltpu.make_async_copy(all_waves, all_ref, load_sem.at[8]),
        pltpu.make_async_copy(back_waves, back_ref, load_sem.at[9]),
    ]
    for load in loads:
        load.start()

    own = ch * sections + sec
    members = range(sections)
    places = [(to_sec, to_ch) for to_ch in range(n_ch) for to_sec in members]
    last, top = sections - 1, n_ch - 1
    opens, closes = sec == 0, sec == last
    middle = jnp.logical_not(jnp.logical_or(opens, closes))
    corner = jnp.logical_and(closes, ch == top)

    def also(one, two):
        return jnp.logical_and(one, two)

    def signal(flag, sem, device):
        @pl.when(flag)
        def _():
            pl.semaphore_signal(sem, inc=1, device_id=device, device_id_type=MESH)

    barrier = pltpu.get_barrier_semaphore()
    signal(middle, barrier, {"sec": last})
    for to_sec in members[1:]:
        signal(opens, barrier, {"sec": to_sec})
    signal(ch < top, barrier, {"sec": last, "ch": top})
    signal(has_after, barrier, {"ctx": ctx + 1})
    heard = (
        middle.astype(jnp.int32)
        + closes.astype(jnp.int32) * last
        + corner.astype(jnp.int32) * (sections * top)
        + has_before.astype(jnp.int32)
    )

    @pl.when(heard > 0)
    def _():
        pl.semaphore_wait(barrier, heard)

    for to_sec in members[:-1]:
        signal(closes, peer_sem.at[last], {"sec": to_sec})
    signal(middle, peer_sem.at[sec], {"sec": 0})
    for to_sec, to_ch in places[:-1]:
        signal(corner, far_sem, {"sec": to_sec, "ch": to_ch})
    signal(has_before, ready_sem, {"ctx": ctx - 1})

    def remote(src, dst, send_sem, recv_sem, device):
        return pltpu.make_async_remote_copy(
            src_ref=src,
            dst_ref=dst,
            send_sem=send_sem,
            recv_sem=recv_sem,
            device_id=device,
            device_id_type=MESH,
        )

    def send_sum(to_sec, to_ch):
        slot = sums_ref.at[own]
        remote(slot, slot, sum_send, sum_recv, {"sec": to_sec, "ch": to_ch}).start()

    def send_field(tables, to_sec):
        field, held, send_sem, recv_sem = tables
        remote(
            field.at[0, :, cut(to_sec)], held.at[sec], send_sem, recv_sem.at[sec], {"sec": to_sec}
        ).start()

    def send_far():
        for to_sec, to_ch in places:

            @pl.when(ch != to_ch)
            def _(to_sec=to_sec, to_ch=to_ch):
                send_sum(to_sec, to_ch)

    def each(flag, chosen, act):
        @pl.when(flag)
        def _():
            for to_sec in chosen:
                act(to_sec)

    leads, follows = ctx % 2 == 0, ctx % 2 == 1
    led = also(leads, has_after)
    keys = key, key_ref, key_send, key_recv
    queries = query, query_ref, query_send, query_recv
    each(middle, members[:1], lambda to_sec: send_field(keys, to_sec))
    each(closes, members[:-1], lambda to_sec: send_field(keys, to_sec))

    loads[0].wait()
    squares = jnp.square(x_ref[...].astype(F32))
    folded = sum(squares[:, low : low + LANES] for low in range(0, width, LANES))
    sums_ref[own] = jnp.sum(folded.T, axis=0, keepdims=True)

    pl.when(corner)(send_far)
    each(middle, members[:1], lambda to_sec: send_sum(to_sec, ch))
    each(closes, members[:-1], lambda to_sec: send_sum(to_sec, ch))

    def meet(to_sec):
        pl.semaphore_wait(peer_sem.at[to_sec], 1)
        send_sum(to_sec, ch)
        send_field(keys, to_sec)

    each(opens, members[1:], meet)

    @pl.when(middle)
    def _():
        pl.semaphore_wait(peer_sem.at[last], 1)

    for act in (lambda to_sec: send_sum(to_sec, ch), lambda to_sec: send_field(keys, to_sec)):
        for to_sec in members[1:]:
            each(also(middle, sec != to_sec), [to_sec], act)
    def send_queries():
        each(opens, members[:0:-1], lambda to_sec: send_field(queries, to_sec))
        for to_sec in members:
            each(also(jnp.logical_not(opens), sec != to_sec), [to_sec], lambda to_sec: send_field(queries, to_sec))

    pl.when(leads)(send_queries)

    def far_sums():
        pl.semaphore_wait(far_sem, 1)
        send_far()

    steps = sec % 2 + sec // 2 + ch
    late = 2 * steps > last % 2 + last // 2 + top
    pl.when(also(late, jnp.logical_not(corner)))(far_sums)

    def arrived(ref, sem):
        pltpu.make_async_copy(ref, ref, sem).wait()

    for load in loads[1:7] + loads[9:]:
        load.wait()
    offsets = row_ids((length, width)).astype(F32)
    ages = (length - 1.0) - offsets
    rate_table = rate_ref[...]
    weights = residue_ref[...] * jnp.sqrt(1.0 - jnp.exp(-2.0 * rate_table))
    taps = jnp.where(row_ids((length, width)) == 0, direct_ref[...], 0.0)
    for mode in range(modes):
        rate = rate_table[mode : mode + 1]
        part = weights[mode : mode + 1] * jnp.exp(-rate * offsets)
        carry_ref[mode] = part
        age_ref[mode] = jnp.exp(-rate * ages)
        taps = taps + part
    decay_ref[0] = jnp.exp(-rate_table)
    decay_ref[1] = jnp.exp(-length * rate_table)
    edge = row_ids((ROWS, width))
    for mode in range(modes):
        rate = rate_table[mode : mode + 1]
        ending_ref[mode] = weights[mode : mode + 1] * jnp.exp(rate * (ROWS - 1.0 - edge.astype(F32)))
    for row in range(ROWS):
        ahead = (row - edge).astype(F32)
        undone = jnp.where(edge == row, direct_ref[...], 0.0)
        for mode in range(modes):
            rate = rate_table[mode : mode + 1]
            gone = weights[mode : mode + 1] * jnp.exp(rate * jnp.maximum(ahead, 0.0))
            undone = undone - jnp.where(ahead > 0, gone, 0.0)
        within_ref[row] = undone
    first = row_ids((length, width)) == 0
    for index, filter_taps in enumerate((medium_ref[...], taps)):
        spectrum = times_parts(own_ref, filter_taps)
        real, imag = spectrum[:length], spectrum[length:]
        spectra_ref[index, 0] = real
        spectra_ref[index, 1] = jnp.where(first, 0.0, imag)
        spectra_ref[index, 2] = jnp.where(first, imag, real)

    scaled_ref[...] = x_ref[...].astype(F32) * gain_ref[...]

    @pl.when(jnp.logical_not(has_before))
    def _():
        padded_ref[:, :, :ROWS] = jnp.zeros((2, len(halves), ROWS, LANES), F32)

    pl.when(jnp.logical_not(late))(far_sums)

    @pl.when(led)
    def _():
        pl.semaphore_wait(ready_sem, 1)
        arrived(key_ref.at[pl.ds(0, sections - 1)], key_send)
        pl.semaphore_signal(turn_sem, inc=1, device_id={"ctx": ctx + 1}, device_id_type=MESH)

    @pl.when(follows)
    def _():
        pl.semaphore_wait(turn_sem, 1)
        send_queries()


    peers = len(places) - 1
    arrived(sums_ref.at[pl.ds(0, peers)], sum_recv)
    total = sums_ref[0]
    for index in range(1, len(places)):
        total = total + sums_ref[index]
    inverse = lax.rsqrt(total / (width * len(places)) + norm_eps)
    scale = jnp.broadcast_to(inverse, (length, length)).T
    for half in halves:
        stream_ref[:, half] = scaled_ref[:, half] * scale

    @pl.when(also(follows, has_after))
    def _():
        pl.semaphore_wait(ready_sem, 1)

    after = {"ctx": lax.rem(ctx + 1, n_ctx)}

    def hand_over(section, src, dst):
        return remote(src, dst, ctx_send.at[section], ctx_recv.at[section], after)

    def gated(section):
        return key_ref[section].astype(F32) * stream_ref[...]

    def advance(section, filtered):
        arrived(query_ref.at[section], query_recv.at[section])
        return stream_ref[...] + query_ref[section].astype(F32) * filtered

    def short_section(section, tap_set):
        values = gated(section)
        for index, half in enumerate(halves):
            padded_ref[tap_set, index, ROWS:] = values[:, half]
        hand = None
        if tap_set:

            @pl.when(has_before)
            def _():
                for index, half in enumerate(halves):
                    padded_ref[tap_set, index, :ROWS] = state_ref[modes:, half]

        else:
            hand = hand_over(
                section,
                padded_ref.at[tap_set, :, pl.ds(length, ROWS)],
                padded_ref.at[tap_set, :, pl.ds(0, ROWS)],
            )

            @pl.when(has_after)
            def _():
                hand.start()

            @pl.when(has_before)
            def _():
                hand.wait_recv()

        filtered = []
        for index, half in enumerate(halves):
            taps = short_ref[:, tap_set, half]
            total = values[:, half] * taps[:1]
            for tap in range(1, taps.shape[0]):
                rows = padded_ref[tap_set, index, pl.ds(ROWS - tap, length)]
                total = total + rows * taps[tap : tap + 1]
            filtered.append(total)
        return hand, advance(section, jnp.concatenate(filtered, axis=1))

    def from_spectrum(index, spectrum):
        real, imag = spectrum[:length], spectrum[length:]
        first, cross, last = (spectra_ref[index, place] for place in range(3))
        product = jnp.concatenate(
            [real * first - imag * cross, real * cross + imag * last], axis=0
        )
        return times(back_ref[...], product)

    def medium_section(section):
        hand = hand_over(section, gated_ref, rows_ref)
        gated_ref[...] = gated(section).astype(BF16)

        @pl.when(has_after)
        def _():
            hand.start()

        arrived(query_ref.at[section], query_recv.at[section])

        def finish(spectrum):
            filtered = from_spectrum(0, spectrum)
            stream_ref[...] += query_ref[section].astype(F32) * filtered

        @pl.when(jnp.logical_not(has_before))
        def _():
            finish(times(own_ref[0], gated_ref[...]))

        @pl.when(has_before)
        def _():
            hand.wait_recv()
            both = jnp.concatenate([gated_ref[...], rows_ref[...]], axis=0)
            finish(times(all_ref[...], both))

        return hand

    def long_section(section):
        hand = hand_over(section, leaving_ref, state_ref)
        values = gated(section)
        arrived(query_ref.at[section], query_recv.at[section])

        arrived(key_ref.at[section + 1], key_recv.at[section + 1])
        end = pl.ds(length - ROWS, ROWS)

        def leave():
            for mode in range(modes):
                leaving_ref[mode : mode + 1] = jnp.sum(
                    age_ref[mode] * values, axis=0, keepdims=True
                )

        def send_end():
            states = leaving_ref[:modes]
            rows = values[length - ROWS :]
            filtered = ending_ref[0] * states[:1]
            for mode in range(1, modes):
                filtered = filtered + ending_ref[mode] * states[mode : mode + 1]
            for row in range(ROWS):
                filtered = filtered + within_ref[row] * rows[row : row + 1]
            stream = stream_ref[end] + query_ref[section, end].astype(F32) * filtered
            leaving_ref[modes:] = key_ref[section + 1, end].astype(F32) * stream
            hand.start()

        @pl.when(jnp.logical_not(has_before))
        def _():
            spectrum = times(own_ref[0], values)
            if n_ctx > 1:
                leave()
                send_end()
            filtered = from_spectrum(1, spectrum)
            stream_ref[...] += query_ref[section].astype(F32) * filtered

        @pl.when(has_before)
        def _():
            filtered = from_spectrum(1, times(own_ref[0], values))
            waiting_ref[...] = stream_ref[...] + query_ref[section].astype(F32) * filtered

            @pl.when(has_after)
            def _():
                leave()

            hand.wait_recv()
            states = state_ref[:modes]

            @pl.when(has_after)
            def _():
                leaving_ref[:modes] += decay_ref[1] * states
                send_end()

            entering = decay_ref[0] * states
            carried = carry_ref[0] * entering[:1]
            for mode in range(1, modes):
                carried = carried + carry_ref[mode] * entering[mode : mode + 1]
            stream_ref[...] = waiting_ref[...] + query_ref[section].astype(F32) * carried

        return hand

    hands = []
    for section in range(sections):
        if section < sections - 1:
            arrived(key_ref.at[section], key_recv.at[section])
        if section == 1:
            hands.append(medium_section(section))
        elif section == 2:
            hands.append(long_section(section))
        else:
            hand, stream = short_section(section, min(section, 1))
            if section:
                out[...] = stream.astype(BF16)
            else:
                hands.append(hand)
                stream_ref[...] = stream

    arrived(sums_ref.at[pl.ds(0, peers)], sum_send)

    @pl.when(jnp.logical_not(led))
    def _():
        arrived(key_ref.at[pl.ds(0, sections - 1)], key_send)

    arrived(query_ref.at[pl.ds(0, sections - 1)], query_send)

    @pl.when(has_after)
    def _():
        for hand in hands:
            hand.wait_send()


def shards(
    inputs,
    query_fields,
    key_fields,
    norm_gain,
    short_taps,
    medium_taps,
    pole_rates,
    pole_residues,
    direct_term,
):
    sections = lax.axis_size("sec")
    n_ctx = lax.axis_size("ctx")
    n_ch = lax.axis_size("ch")
    length, width = inputs.shape
    modes = pole_rates.shape[0]
    shorts, short_span = short_taps.shape[:2]
    tables = waves(length)
    anywhere = pl.BlockSpec(memory_space=pl.ANY)
    dma = pltpu.SemaphoreType.DMA
    return pl.pallas_call(
        functools.partial(kernel, sections, n_ctx, n_ch),
        out_shape=jax.ShapeDtypeStruct((length, width), inputs.dtype),
        in_specs=[anywhere] * 12,
        out_specs=pl.BlockSpec(memory_space=pltpu.VMEM),
        scratch_shapes=[
            pltpu.VMEM((length, width), inputs.dtype),
            pltpu.VMEM((1, width), F32),
            pltpu.VMEM((short_span, shorts, width), F32),
            pltpu.VMEM((medium_taps.shape[0], width), F32),
            pltpu.VMEM((modes, width), F32),
            pltpu.VMEM((modes, width), F32),
            pltpu.VMEM((1, width), F32),
            pltpu.VMEM((sections, length, width), key_fields.dtype),
            pltpu.VMEM((sections, length, width), query_fields.dtype),
            pltpu.VMEM((n_ch * sections, 1, length), F32),
            pltpu.VMEM((2, width // LANES, ROWS + length, LANES), F32),
            pltpu.VMEM((length, width), BF16),
            pltpu.VMEM((length, width), BF16),
            pltpu.VMEM((length, width), F32),
            pltpu.VMEM((length, width), F32),
            pltpu.VMEM((length, width), F32),
            pltpu.VMEM((modes + ROWS, width), F32),
            pltpu.VMEM((modes + ROWS, width), F32),
            pltpu.VMEM((modes, length, width), F32),
            pltpu.VMEM((modes, length, width), F32),
            pltpu.VMEM((2, modes, width), F32),
            pltpu.VMEM((modes, ROWS, width), F32),
            pltpu.VMEM((ROWS, ROWS, width), F32),
            pltpu.VMEM(tables[0].shape, BF16),
            pltpu.VMEM(tables[1].shape, BF16),
            pltpu.VMEM(tables[2].shape, BF16),
            pltpu.VMEM((2, 3, length, width), F32),
            dma((10,)),
            dma,
            dma((sections,)),
            dma,
            dma((sections,)),
            dma,
            dma,
            dma((sections,)),
            dma((sections,)),
            pltpu.SemaphoreType.REGULAR((sections,)),
            pltpu.SemaphoreType.REGULAR,
            pltpu.SemaphoreType.REGULAR,
            pltpu.SemaphoreType.REGULAR,
        ],
        compiler_params=pltpu.CompilerParams(collective_id=0, has_side_effects=True, vmem_limit_bytes=8*2**20),
    )(*[pltpu.with_memory_space_constraint(a, pltpu.HBM) for a in (
        inputs,
        query_fields,
        key_fields,
        norm_gain[None],
        jnp.swapaxes(short_taps, 0, 1),
        medium_taps,
        pole_rates,
        pole_residues,
        direct_term[None],
        *(jnp.asarray(table) for table in tables),
    )])


def solution(mesh):
    in_specs = (
        P("ctx", ("ch", "sec")),
        P("sec", "ctx", "ch"),
        P("sec", "ctx", "ch"),
        P("ch"),
        P(None, None, "ch"),
        P(None, "ch"),
        P(None, "ch"),
        P(None, "ch"),
        P("ch"),
    )
    out_specs = P("ctx", ("ch", "sec"))
    return jax.shard_map(shards, mesh=mesh, in_specs=in_specs, out_specs=out_specs, check_vma=False)
```

```python
import functools

import jax
import jax.numpy as jnp
import numpy as np
from jax import lax
from jax.experimental import pallas as pl
from jax.experimental.pallas import tpu as pltpu
from jax.sharding import PartitionSpec as P

norm_eps = 1e-06
MESH = pl.DeviceIdType.MESH
LANES = 128
ROWS = 8
F32 = jnp.float32
BF16 = jnp.bfloat16


def row_ids(shape):
    return lax.broadcasted_iota(jnp.int32, shape, 0)


def parts(values):
    high = values.astype(BF16)
    return high, (values - high.astype(F32)).astype(BF16)


def times(table, values):
    values = values.astype(BF16)
    half = table.shape[0] // 2
    return jnp.concatenate(
        [
            jnp.dot(rows, values, preferred_element_type=F32)
            for rows in (table[:half], table[half:])
        ],
        axis=0,
    )


def times_parts(table, values):
    high, low = parts(values)
    return times(table[0], high) + times(table[0], low) + times(table[1], high)


def waves(length):
    size = 2 * length
    order = np.arange(length)
    turn = 2 * np.pi * np.outer(order, np.arange(size)) / size
    ends = np.cos(np.pi * np.arange(size))
    real, imag = np.cos(turn), -np.sin(turn)
    imag[0] = ends
    back_real, back_imag = 2 * real.T / size, 2 * imag.T / size
    back_real[:, 0] /= 2
    back_imag[:, 0] /= 2
    ahead = np.concatenate([real, imag], axis=0)
    back = np.concatenate([back_real, back_imag], axis=1)[:length]
    own = ahead[:, :length]
    high = own.astype(BF16)
    low = (own - high.astype(np.float64)).astype(BF16)
    return np.stack([high, low]), ahead.astype(BF16), back.astype(BF16)


def kernel(
    sections,
    n_ctx,
    n_ch,
    inputs,
    query,
    key,
    gain,
    short,
    medium,
    rates,
    residues,
    direct,
    own_waves,
    all_waves,
    back_waves,
    out,
    x_ref,
    gain_ref,
    short_ref,
    medium_ref,
    rate_ref,
    residue_ref,
    direct_ref,
    key_ref,
    query_ref,
    sums_ref,
    padded_ref,
    gated_ref,
    rows_ref,
    scaled_ref,
    stream_ref,
    keyed_ref,
    waiting_ref,
    state_ref,
    leaving_ref,
    age_ref,
    carry_ref,
    decay_ref,
    ending_ref,
    within_ref,
    own_ref,
    all_ref,
    back_ref,
    spectra_ref,
    load_sem,
    key_send,
    key_recv,
    query_send,
    query_recv,
    sum_send,
    sum_recv,
    ctx_send,
    ctx_recv,
    peer_sem,
    far_sem,
    ready_sem,
    turn_sem,
):
    length, width = x_ref.shape
    modes = rate_ref.shape[0]
    sec = lax.axis_index("sec")
    ctx = lax.axis_index("ctx")
    ch = lax.axis_index("ch")
    has_before = ctx > 0
    has_after = ctx < n_ctx - 1

    def cut(index):
        return pl.ds(pl.multiple_of(index * width, width), width)

    mine = cut(sec)
    halves = [slice(low, low + LANES) for low in range(0, width, LANES)]
    loads = [
        pltpu.make_async_copy(inputs, x_ref, load_sem.at[0]),
        pltpu.make_async_copy(rates.at[:, mine], rate_ref, load_sem.at[1]),
        pltpu.make_async_copy(residues.at[:, mine], residue_ref, load_sem.at[2]),
        pltpu.make_async_copy(direct.at[:, mine], direct_ref, load_sem.at[3]),
        pltpu.make_async_copy(gain.at[:, mine], gain_ref, load_sem.at[4]),
        pltpu.make_async_copy(short.at[:, :, mine], short_ref, load_sem.at[5]),
        pltpu.make_async_copy(medium.at[:, mine], medium_ref, load_sem.at[6]),
        pltpu.make_async_copy(key.at[0, :, mine], key_ref.at[sec], key_recv.at[sec]),
        pltpu.make_async_copy(query.at[0, :, mine], query_ref.at[sec], query_recv.at[sec]),
        pltpu.make_async_copy(own_waves, own_ref, load_sem.at[7]),
        pltpu.make_async_copy(all_waves, all_ref, load_sem.at[8]),
        pltpu.make_async_copy(back_waves, back_ref, load_sem.at[9]),
    ]
    for load in loads:
        load.start()

    own = ch * sections + sec
    members = range(sections)
    places = [(to_sec, to_ch) for to_ch in range(n_ch) for to_sec in members]
    last, top = sections - 1, n_ch - 1
    opens, closes = sec == 0, sec == last
    middle = jnp.logical_not(jnp.logical_or(opens, closes))
    corner = jnp.logical_and(closes, ch == top)

    def also(one, two):
        return jnp.logical_and(one, two)

    def signal(flag, sem, device):
        @pl.when(flag)
        def _():
            pl.semaphore_signal(sem, inc=1, device_id=device, device_id_type=MESH)

    barrier = pltpu.get_barrier_semaphore()
    signal(middle, barrier, {"sec": last})
    for to_sec in members[1:]:
        signal(opens, barrier, {"sec": to_sec})
    signal(ch < top, barrier, {"sec": last, "ch": top})
    signal(has_after, barrier, {"ctx": ctx + 1})
    heard = (
        middle.astype(jnp.int32)
        + closes.astype(jnp.int32) * last
        + corner.astype(jnp.int32) * (sections * top)
        + has_before.astype(jnp.int32)
    )

    @pl.when(heard > 0)
    def _():
        pl.semaphore_wait(barrier, heard)

    for to_sec in members[:-1]:
        signal(closes, peer_sem.at[last], {"sec": to_sec})
    signal(middle, peer_sem.at[sec], {"sec": 0})
    for to_sec, to_ch in places[:-1]:
        signal(corner, far_sem, {"sec": to_sec, "ch": to_ch})
    signal(has_before, ready_sem, {"ctx": ctx - 1})

    def remote(src, dst, send_sem, recv_sem, device):
        return pltpu.make_async_remote_copy(
            src_ref=src,
            dst_ref=dst,
            send_sem=send_sem,
            recv_sem=recv_sem,
            device_id=device,
            device_id_type=MESH,
        )

    def send_sum(to_sec, to_ch):
        slot = sums_ref.at[own]
        remote(slot, slot, sum_send, sum_recv, {"sec": to_sec, "ch": to_ch}).start()

    def send_field(tables, to_sec):
        field, held, send_sem, recv_sem = tables
        remote(
            field.at[0, :, cut(to_sec)], held.at[sec], send_sem, recv_sem.at[sec], {"sec": to_sec}
        ).start()

    def send_far():
        for to_sec, to_ch in places:

            @pl.when(ch != to_ch)
            def _(to_sec=to_sec, to_ch=to_ch):
                send_sum(to_sec, to_ch)

    def each(flag, chosen, act):
        @pl.when(flag)
        def _():
            for to_sec in chosen:
                act(to_sec)

    leads, follows = ctx % 2 == 0, ctx % 2 == 1
    led = also(leads, has_after)
    keys = key, key_ref, key_send, key_recv
    queries = query, query_ref, query_send, query_recv
    each(middle, members[:1], lambda to_sec: send_field(keys, to_sec))
    each(closes, members[:-1], lambda to_sec: send_field(keys, to_sec))

    loads[0].wait()
    squares = jnp.square(x_ref[...].astype(F32))
    folded = sum(squares[:, low : low + LANES] for low in range(0, width, LANES))
    sums_ref[own] = jnp.sum(folded.T, axis=0, keepdims=True)

    pl.when(corner)(send_far)
    each(middle, members[:1], lambda to_sec: send_sum(to_sec, ch))
    each(closes, members[:-1], lambda to_sec: send_sum(to_sec, ch))

    def meet(to_sec):
        pl.semaphore_wait(peer_sem.at[to_sec], 1)
        send_sum(to_sec, ch)
        send_field(keys, to_sec)

    each(opens, members[1:], meet)

    @pl.when(middle)
    def _():
        pl.semaphore_wait(peer_sem.at[last], 1)

    for act in (lambda to_sec: send_sum(to_sec, ch), lambda to_sec: send_field(keys, to_sec)):
        for to_sec in members[1:]:
            each(also(middle, sec != to_sec), [to_sec], act)
    def send_queries():
        each(opens, members[:0:-1], lambda to_sec: send_field(queries, to_sec))
        for to_sec in members:
            each(also(jnp.logical_not(opens), sec != to_sec), [to_sec], lambda to_sec: send_field(queries, to_sec))

    pl.when(leads)(send_queries)

    def far_sums():
        pl.semaphore_wait(far_sem, 1)
        send_far()

    steps = sec % 2 + sec // 2 + ch
    late = 2 * steps > last % 2 + last // 2 + top
    pl.when(also(late, jnp.logical_not(corner)))(far_sums)

    def arrived(ref, sem):
        pltpu.make_async_copy(ref, ref, sem).wait()

    for load in loads[1:7] + loads[9:]:
        load.wait()
    offsets = row_ids((length, width)).astype(F32)
    ages = (length - 1.0) - offsets
    rate_table = rate_ref[...]
    weights = residue_ref[...] * jnp.sqrt(1.0 - jnp.exp(-2.0 * rate_table))
    taps = jnp.where(row_ids((length, width)) == 0, direct_ref[...], 0.0)
    for mode in range(modes):
        rate = rate_table[mode : mode + 1]
        part = weights[mode : mode + 1] * jnp.exp(-rate * offsets)
        carry_ref[mode] = part
        age_ref[mode] = jnp.exp(-rate * ages)
        taps = taps + part
    decay_ref[0] = jnp.exp(-rate_table)
    decay_ref[1] = jnp.exp(-length * rate_table)
    edge = row_ids((ROWS, width))
    for mode in range(modes):
        rate = rate_table[mode : mode + 1]
        ending_ref[mode] = weights[mode : mode + 1] * jnp.exp(rate * (ROWS - 1.0 - edge.astype(F32)))
    for row in range(ROWS):
        ahead = (row - edge).astype(F32)
        undone = jnp.where(edge == row, direct_ref[...], 0.0)
        for mode in range(modes):
            rate = rate_table[mode : mode + 1]
            gone = weights[mode : mode + 1] * jnp.exp(rate * jnp.maximum(ahead, 0.0))
            undone = undone - jnp.where(ahead > 0, gone, 0.0)
        within_ref[row] = undone
    first = row_ids((length, width)) == 0
    for index, filter_taps in enumerate((medium_ref[...], taps)):
        spectrum = times_parts(own_ref, filter_taps)
        real, imag = spectrum[:length], spectrum[length:]
        spectra_ref[index, 0] = real
        spectra_ref[index, 1] = jnp.where(first, 0.0, imag)
        spectra_ref[index, 2] = jnp.where(first, imag, real)

    scaled_ref[...] = x_ref[...].astype(F32) * gain_ref[...]

    @pl.when(jnp.logical_not(has_before))
    def _():
        padded_ref[:, :, :ROWS] = jnp.zeros((2, len(halves), ROWS, LANES), F32)

    pl.when(jnp.logical_not(late))(far_sums)

    @pl.when(led)
    def _():
        pl.semaphore_wait(ready_sem, 1)
        arrived(key_ref.at[pl.ds(0, sections - 1)], key_send)
        pl.semaphore_signal(turn_sem, inc=1, device_id={"ctx": ctx + 1}, device_id_type=MESH)

    @pl.when(follows)
    def _():
        pl.semaphore_wait(turn_sem, 1)
        send_queries()


    arrived(key_ref.at[0], key_recv.at[0])
    keyed_ref[...] = scaled_ref[...] * key_ref[0].astype(F32)
    peers = len(places) - 1
    arrived(sums_ref.at[pl.ds(0, peers)], sum_recv)
    totals = [sums_ref[index] for index in range(len(places))]
    while len(totals) > 1:
        odd = totals[len(totals) // 2 * 2 :]
        totals = [one + two for one, two in zip(totals[::2], totals[1::2])] + odd
    inverse = lax.rsqrt(totals[0] / (width * len(places)) + norm_eps)
    scale = jnp.broadcast_to(inverse, (length, length)).T
    for index, half in enumerate(halves):
        padded_ref[0, index, ROWS:] = keyed_ref[:, half] * scale
        stream_ref[:, half] = scaled_ref[:, half] * scale

    @pl.when(also(follows, has_after))
    def _():
        pl.semaphore_wait(ready_sem, 1)

    after = {"ctx": lax.rem(ctx + 1, n_ctx)}

    def hand_over(section, src, dst):
        return remote(src, dst, ctx_send.at[section], ctx_recv.at[section], after)

    def gated(section):
        return key_ref[section].astype(F32) * stream_ref[...]

    def advance(section, filtered):
        arrived(query_ref.at[section], query_recv.at[section])
        return stream_ref[...] + query_ref[section].astype(F32) * filtered

    def short_section(section, tap_set):
        hand = None
        if tap_set:
            values = gated(section)
            for index, half in enumerate(halves):
                padded_ref[tap_set, index, ROWS:] = values[:, half]

            @pl.when(has_before)
            def _():
                for index, half in enumerate(halves):
                    padded_ref[tap_set, index, :ROWS] = state_ref[modes:, half]

        else:
            hand = hand_over(
                section,
                padded_ref.at[tap_set, :, pl.ds(length, ROWS)],
                padded_ref.at[tap_set, :, pl.ds(0, ROWS)],
            )

            @pl.when(has_after)
            def _():
                hand.start()

            @pl.when(has_before)
            def _():
                hand.wait_recv()

        filtered = []
        for index, half in enumerate(halves):
            taps = short_ref[:, tap_set, half]
            total = padded_ref[tap_set, index, pl.ds(ROWS, length)] * taps[:1]
            for tap in range(1, taps.shape[0]):
                rows = padded_ref[tap_set, index, pl.ds(ROWS - tap, length)]
                total = total + rows * taps[tap : tap + 1]
            filtered.append(total)
        return hand, advance(section, jnp.concatenate(filtered, axis=1))

    def from_spectrum(index, spectrum):
        real, imag = spectrum[:length], spectrum[length:]
        first, cross, last = (spectra_ref[index, place] for place in range(3))
        product = jnp.concatenate(
            [real * first - imag * cross, real * cross + imag * last], axis=0
        )
        return times(back_ref[...], product)

    def medium_section(section):
        hand = hand_over(section, gated_ref, rows_ref)
        gated_ref[...] = gated(section).astype(BF16)

        @pl.when(has_after)
        def _():
            hand.start()

        arrived(query_ref.at[section], query_recv.at[section])

        def finish(spectrum):
            filtered = from_spectrum(0, spectrum)
            stream_ref[...] += query_ref[section].astype(F32) * filtered

        @pl.when(jnp.logical_not(has_before))
        def _():
            finish(times(own_ref[0], gated_ref[...]))

        @pl.when(has_before)
        def _():
            hand.wait_recv()
            both = jnp.concatenate([gated_ref[...], rows_ref[...]], axis=0)
            finish(times(all_ref[...], both))

        return hand

    def long_section(section):
        hand = hand_over(section, leaving_ref, state_ref)
        values = gated(section)
        arrived(query_ref.at[section], query_recv.at[section])

        arrived(key_ref.at[section + 1], key_recv.at[section + 1])
        end = pl.ds(length - ROWS, ROWS)

        def leave():
            for mode in range(modes):
                leaving_ref[mode : mode + 1] = jnp.sum(
                    age_ref[mode] * values, axis=0, keepdims=True
                )

        def send_end():
            states = leaving_ref[:modes]
            rows = values[length - ROWS :]
            filtered = ending_ref[0] * states[:1]
            for mode in range(1, modes):
                filtered = filtered + ending_ref[mode] * states[mode : mode + 1]
            for row in range(ROWS):
                filtered = filtered + within_ref[row] * rows[row : row + 1]
            stream = stream_ref[end] + query_ref[section, end].astype(F32) * filtered
            leaving_ref[modes:] = key_ref[section + 1, end].astype(F32) * stream
            hand.start()

        @pl.when(jnp.logical_not(has_before))
        def _():
            spectrum = times(own_ref[0], values)
            if n_ctx > 1:
                leave()
                send_end()
            filtered = from_spectrum(1, spectrum)
            stream_ref[...] += query_ref[section].astype(F32) * filtered

        @pl.when(has_before)
        def _():
            filtered = from_spectrum(1, times(own_ref[0], values))
            waiting_ref[...] = stream_ref[...] + query_ref[section].astype(F32) * filtered

            @pl.when(has_after)
            def _():
                leave()

            hand.wait_recv()
            states = state_ref[:modes]

            @pl.when(has_after)
            def _():
                leaving_ref[:modes] += decay_ref[1] * states
                send_end()

            entering = decay_ref[0] * states
            carried = carry_ref[0] * entering[:1]
            for mode in range(1, modes):
                carried = carried + carry_ref[mode] * entering[mode : mode + 1]
            stream_ref[...] = waiting_ref[...] + query_ref[section].astype(F32) * carried

        return hand

    hands = []
    for section in range(sections):
        if 0 < section < sections - 1:
            arrived(key_ref.at[section], key_recv.at[section])
        if section == 1:
            hands.append(medium_section(section))
        elif section == 2:
            hands.append(long_section(section))
        else:
            hand, stream = short_section(section, min(section, 1))
            if section:
                out[...] = stream.astype(BF16)
            else:
                hands.append(hand)
                stream_ref[...] = stream

    arrived(sums_ref.at[pl.ds(0, peers)], sum_send)

    @pl.when(jnp.logical_not(led))
    def _():
        arrived(key_ref.at[pl.ds(0, sections - 1)], key_send)

    arrived(query_ref.at[pl.ds(0, sections - 1)], query_send)

    @pl.when(has_after)
    def _():
        for hand in hands:
            hand.wait_send()


def shards(
    inputs,
    query_fields,
    key_fields,
    norm_gain,
    short_taps,
    medium_taps,
    pole_rates,
    pole_residues,
    direct_term,
):
    sections = lax.axis_size("sec")
    n_ctx = lax.axis_size("ctx")
    n_ch = lax.axis_size("ch")
    length, width = inputs.shape
    modes = pole_rates.shape[0]
    shorts, short_span = short_taps.shape[:2]
    tables = waves(length)
    anywhere = pl.BlockSpec(memory_space=pl.ANY)
    dma = pltpu.SemaphoreType.DMA
    return pl.pallas_call(
        functools.partial(kernel, sections, n_ctx, n_ch),
        out_shape=jax.ShapeDtypeStruct((length, width), inputs.dtype),
        in_specs=[anywhere] * 12,
        out_specs=pl.BlockSpec(memory_space=pltpu.VMEM),
        scratch_shapes=[
            pltpu.VMEM((length, width), inputs.dtype),
            pltpu.VMEM((1, width), F32),
            pltpu.VMEM((short_span, shorts, width), F32),
            pltpu.VMEM((medium_taps.shape[0], width), F32),
            pltpu.VMEM((modes, width), F32),
            pltpu.VMEM((modes, width), F32),
            pltpu.VMEM((1, width), F32),
            pltpu.VMEM((sections, length, width), key_fields.dtype),
            pltpu.VMEM((sections, length, width), query_fields.dtype),
            pltpu.VMEM((n_ch * sections, 1, length), F32),
            pltpu.VMEM((2, width // LANES, ROWS + length, LANES), F32),
            pltpu.VMEM((length, width), BF16),
            pltpu.VMEM((length, width), BF16),
            pltpu.VMEM((length, width), F32),
            pltpu.VMEM((length, width), F32),
            pltpu.VMEM((length, width), F32),
            pltpu.VMEM((length, width), F32),
            pltpu.VMEM((modes + ROWS, width), F32),
            pltpu.VMEM((modes + ROWS, width), F32),
            pltpu.VMEM((modes, length, width), F32),
            pltpu.VMEM((modes, length, width), F32),
            pltpu.VMEM((2, modes, width), F32),
            pltpu.VMEM((modes, ROWS, width), F32),
            pltpu.VMEM((ROWS, ROWS, width), F32),
            pltpu.VMEM(tables[0].shape, BF16),
            pltpu.VMEM(tables[1].shape, BF16),
            pltpu.VMEM(tables[2].shape, BF16),
            pltpu.VMEM((2, 3, length, width), F32),
            dma((10,)),
            dma,
            dma((sections,)),
            dma,
            dma((sections,)),
            dma,
            dma,
            dma((sections,)),
            dma((sections,)),
            pltpu.SemaphoreType.REGULAR((sections,)),
            pltpu.SemaphoreType.REGULAR,
            pltpu.SemaphoreType.REGULAR,
            pltpu.SemaphoreType.REGULAR,
        ],
        compiler_params=pltpu.CompilerParams(collective_id=0, has_side_effects=True, vmem_limit_bytes=8*2**20),
    )(*[pltpu.with_memory_space_constraint(a, pltpu.HBM) for a in (
        inputs,
        query_fields,
        key_fields,
        norm_gain[None],
        jnp.swapaxes(short_taps, 0, 1),
        medium_taps,
        pole_rates,
        pole_residues,
        direct_term[None],
        *(jnp.asarray(table) for table in tables),
    )])


def solution(mesh):
    in_specs = (
        P("ctx", ("ch", "sec")),
        P("sec", "ctx", "ch"),
        P("sec", "ctx", "ch"),
        P("ch"),
        P(None, None, "ch"),
        P(None, "ch"),
        P(None, "ch"),
        P(None, "ch"),
        P("ch"),
    )
    out_specs = P("ctx", ("ch", "sec"))
    return jax.shard_map(shards, mesh=mesh, in_specs=in_specs, out_specs=out_specs, check_vma=False)
```

```python
import functools

import jax
import jax.numpy as jnp
import numpy as np
from jax import lax
from jax.experimental import pallas as pl
from jax.experimental.pallas import tpu as pltpu
from jax.sharding import PartitionSpec as P

norm_eps = 1e-06
MESH = pl.DeviceIdType.MESH
LANES = 128
ROWS = 8
F32 = jnp.float32
BF16 = jnp.bfloat16


def row_ids(shape):
    return lax.broadcasted_iota(jnp.int32, shape, 0)


def parts(values):
    high = values.astype(BF16)
    return high, (values - high.astype(F32)).astype(BF16)


def times(table, values):
    values = values.astype(BF16)
    half = table.shape[0] // 2
    return jnp.concatenate(
        [
            jnp.dot(rows, values, preferred_element_type=F32)
            for rows in (table[:half], table[half:])
        ],
        axis=0,
    )


def times_parts(table, values):
    high, low = parts(values)
    return times(table[0], high) + times(table[0], low) + times(table[1], high)


def waves(length):
    size = 2 * length
    order = np.arange(length)
    turn = 2 * np.pi * np.outer(order, np.arange(size)) / size
    ends = np.cos(np.pi * np.arange(size))
    real, imag = np.cos(turn), -np.sin(turn)
    imag[0] = ends
    back_real, back_imag = 2 * real.T / size, 2 * imag.T / size
    back_real[:, 0] /= 2
    back_imag[:, 0] /= 2
    ahead = np.concatenate([real, imag], axis=0)
    back = np.concatenate([back_real, back_imag], axis=1)[:length]
    own = ahead[:, :length]
    high = own.astype(BF16)
    low = (own - high.astype(np.float64)).astype(BF16)
    return np.stack([high, low]), ahead.astype(BF16), back.astype(BF16)


def kernel(
    sections,
    n_ctx,
    n_ch,
    inputs,
    query,
    key,
    gain,
    short,
    medium,
    rates,
    residues,
    direct,
    own_waves,
    all_waves,
    back_waves,
    out,
    x_ref,
    gain_ref,
    short_ref,
    medium_ref,
    rate_ref,
    residue_ref,
    direct_ref,
    key_ref,
    query_ref,
    sums_ref,
    padded_ref,
    gated_ref,
    rows_ref,
    scaled_ref,
    stream_ref,
    waiting_ref,
    state_ref,
    leaving_ref,
    age_ref,
    carry_ref,
    decay_ref,
    ending_ref,
    within_ref,
    own_ref,
    all_ref,
    back_ref,
    spectra_ref,
    load_sem,
    key_send,
    key_recv,
    query_send,
    query_recv,
    sum_send,
    sum_recv,
    ctx_send,
    ctx_recv,
    peer_sem,
    far_sem,
    ready_sem,
    turn_sem,
):
    length, width = x_ref.shape
    modes = rate_ref.shape[0]
    sec = lax.axis_index("sec")
    ctx = lax.axis_index("ctx")
    ch = lax.axis_index("ch")
    has_before = ctx > 0
    has_after = ctx < n_ctx - 1

    def cut(index):
        return pl.ds(pl.multiple_of(index * width, width), width)

    mine = cut(sec)
    halves = [slice(low, low + LANES) for low in range(0, width, LANES)]
    loads = [
        pltpu.make_async_copy(inputs, x_ref, load_sem.at[0]),
        pltpu.make_async_copy(rates.at[:, mine], rate_ref, load_sem.at[1]),
        pltpu.make_async_copy(residues.at[:, mine], residue_ref, load_sem.at[2]),
        pltpu.make_async_copy(direct.at[:, mine], direct_ref, load_sem.at[3]),
        pltpu.make_async_copy(gain.at[:, mine], gain_ref, load_sem.at[4]),
        pltpu.make_async_copy(short.at[:, :, mine], short_ref, load_sem.at[5]),
        pltpu.make_async_copy(medium.at[:, mine], medium_ref, load_sem.at[6]),
        pltpu.make_async_copy(key.at[0, :, mine], key_ref.at[sec], key_recv.at[sec]),
        pltpu.make_async_copy(query.at[0, :, mine], query_ref.at[sec], query_recv.at[sec]),
        pltpu.make_async_copy(own_waves, own_ref, load_sem.at[7]),
        pltpu.make_async_copy(all_waves, all_ref, load_sem.at[8]),
        pltpu.make_async_copy(back_waves, back_ref, load_sem.at[9]),
    ]
    for load in loads:
        load.start()

    own = ch * sections + sec
    members = range(sections)
    places = [(to_sec, to_ch) for to_ch in range(n_ch) for to_sec in members]
    last, top = sections - 1, n_ch - 1
    opens, closes = sec == 0, sec == last
    middle = jnp.logical_not(jnp.logical_or(opens, closes))
    corner = jnp.logical_and(closes, ch == top)

    def also(one, two):
        return jnp.logical_and(one, two)

    def signal(flag, sem, device):
        @pl.when(flag)
        def _():
            pl.semaphore_signal(sem, inc=1, device_id=device, device_id_type=MESH)

    barrier = pltpu.get_barrier_semaphore()
    signal(middle, barrier, {"sec": last})
    for to_sec in members[1:]:
        signal(opens, barrier, {"sec": to_sec})
    signal(ch < top, barrier, {"sec": last, "ch": top})
    signal(has_after, barrier, {"ctx": ctx + 1})
    heard = (
        middle.astype(jnp.int32)
        + closes.astype(jnp.int32) * last
        + corner.astype(jnp.int32) * (sections * top)
        + has_before.astype(jnp.int32)
    )

    @pl.when(heard > 0)
    def _():
        pl.semaphore_wait(barrier, heard)

    for to_sec in members[:-1]:
        signal(closes, peer_sem.at[last], {"sec": to_sec})
    signal(middle, peer_sem.at[sec], {"sec": 0})
    for to_sec, to_ch in places[:-1]:
        signal(corner, far_sem, {"sec": to_sec, "ch": to_ch})
    signal(has_before, ready_sem, {"ctx": ctx - 1})

    def remote(src, dst, send_sem, recv_sem, device):
        return pltpu.make_async_remote_copy(
            src_ref=src,
            dst_ref=dst,
            send_sem=send_sem,
            recv_sem=recv_sem,
            device_id=device,
            device_id_type=MESH,
        )

    def send_sum(to_sec, to_ch):
        slot = sums_ref.at[own]
        remote(slot, slot, sum_send, sum_recv, {"sec": to_sec, "ch": to_ch}).start()

    def send_field(tables, to_sec):
        field, held, send_sem, recv_sem = tables
        remote(
            field.at[0, :, cut(to_sec)], held.at[sec], send_sem, recv_sem.at[sec], {"sec": to_sec}
        ).start()

    def send_far():
        for to_sec, to_ch in places:

            @pl.when(ch != to_ch)
            def _(to_sec=to_sec, to_ch=to_ch):
                send_sum(to_sec, to_ch)

    def each(flag, chosen, act):
        @pl.when(flag)
        def _():
            for to_sec in chosen:
                act(to_sec)

    leads, follows = ctx % 2 == 0, ctx % 2 == 1
    led = also(leads, has_after)
    keys = key, key_ref, key_send, key_recv
    queries = query, query_ref, query_send, query_recv
    each(middle, members[:1], lambda to_sec: send_field(keys, to_sec))
    each(closes, members[:-1], lambda to_sec: send_field(keys, to_sec))

    loads[0].wait()
    squares = jnp.square(x_ref[...].astype(F32))
    folded = sum(squares[:, low : low + LANES] for low in range(0, width, LANES))
    sums_ref[own] = jnp.sum(folded.T, axis=0, keepdims=True)

    pl.when(corner)(send_far)
    each(middle, members[:1], lambda to_sec: send_sum(to_sec, ch))
    each(closes, members[:-1], lambda to_sec: send_sum(to_sec, ch))

    def meet(to_sec):
        pl.semaphore_wait(peer_sem.at[to_sec], 1)
        send_sum(to_sec, ch)
        send_field(keys, to_sec)

    each(opens, members[1:], meet)

    @pl.when(middle)
    def _():
        pl.semaphore_wait(peer_sem.at[last], 1)

    for act in (lambda to_sec: send_sum(to_sec, ch), lambda to_sec: send_field(keys, to_sec)):
        for to_sec in members[1:]:
            each(also(middle, sec != to_sec), [to_sec], act)
    def send_queries():
        each(opens, members[:0:-1], lambda to_sec: send_field(queries, to_sec))
        for to_sec in members:
            each(also(jnp.logical_not(opens), sec != to_sec), [to_sec], lambda to_sec: send_field(queries, to_sec))

    pl.when(leads)(send_queries)

    def far_sums():
        pl.semaphore_wait(far_sem, 1)
        send_far()

    steps = sec % 2 + sec // 2 + ch
    late = 2 * steps > last % 2 + last // 2 + top
    pl.when(also(late, jnp.logical_not(corner)))(far_sums)

    def arrived(ref, sem):
        pltpu.make_async_copy(ref, ref, sem).wait()

    for load in loads[1:7] + loads[9:]:
        load.wait()
    offsets = row_ids((length, width)).astype(F32)
    ages = (length - 1.0) - offsets
    rate_table = rate_ref[...]
    weights = residue_ref[...] * jnp.sqrt(1.0 - jnp.exp(-2.0 * rate_table))
    taps = jnp.where(row_ids((length, width)) == 0, direct_ref[...], 0.0)
    for mode in range(modes):
        rate = rate_table[mode : mode + 1]
        part = weights[mode : mode + 1] * jnp.exp(-rate * offsets)
        carry_ref[mode] = part
        age_ref[mode] = jnp.exp(-rate * ages)
        taps = taps + part
    decay_ref[0] = jnp.exp(-rate_table)
    decay_ref[1] = jnp.exp(-length * rate_table)
    edge = row_ids((ROWS, width))
    for mode in range(modes):
        rate = rate_table[mode : mode + 1]
        ending_ref[mode] = weights[mode : mode + 1] * jnp.exp(rate * (ROWS - 1.0 - edge.astype(F32)))
    for row in range(ROWS):
        ahead = (row - edge).astype(F32)
        undone = jnp.where(edge == row, direct_ref[...], 0.0)
        for mode in range(modes):
            rate = rate_table[mode : mode + 1]
            gone = weights[mode : mode + 1] * jnp.exp(rate * jnp.maximum(ahead, 0.0))
            undone = undone - jnp.where(ahead > 0, gone, 0.0)
        within_ref[row] = undone
    first = row_ids((length, width)) == 0
    for index, filter_taps in enumerate((medium_ref[...], taps)):
        spectrum = times_parts(own_ref, filter_taps)
        real, imag = spectrum[:length], spectrum[length:]
        spectra_ref[index, 0] = real
        spectra_ref[index, 1] = jnp.where(first, 0.0, imag)
        spectra_ref[index, 2] = jnp.where(first, imag, real)

    scaled_ref[...] = x_ref[...].astype(F32) * gain_ref[...]

    @pl.when(jnp.logical_not(has_before))
    def _():
        padded_ref[:, :, :ROWS] = jnp.zeros((2, len(halves), ROWS, LANES), F32)

    pl.when(jnp.logical_not(late))(far_sums)

    @pl.when(led)
    def _():
        pl.semaphore_wait(ready_sem, 1)
        arrived(key_ref.at[pl.ds(0, sections - 1)], key_send)
        pl.semaphore_signal(turn_sem, inc=1, device_id={"ctx": ctx + 1}, device_id_type=MESH)

    @pl.when(follows)
    def _():
        pl.semaphore_wait(turn_sem, 1)
        send_queries()


    peers = len(places) - 1
    arrived(sums_ref.at[pl.ds(0, peers)], sum_recv)
    total = sums_ref[0]
    for index in range(1, len(places)):
        total = total + sums_ref[index]
    inverse = lax.rsqrt(total / (width * len(places)) + norm_eps)
    scale = jnp.broadcast_to(inverse, (length, length)).T
    for half in halves:
        stream_ref[:, half] = scaled_ref[:, half] * scale

    @pl.when(also(follows, has_after))
    def _():
        pl.semaphore_wait(ready_sem, 1)

    after = {"ctx": lax.rem(ctx + 1, n_ctx)}

    def hand_over(section, src, dst):
        return remote(src, dst, ctx_send.at[section], ctx_recv.at[section], after)

    def gated(section):
        return key_ref[section].astype(F32) * stream_ref[...]

    def advance(section, filtered):
        arrived(query_ref.at[section], query_recv.at[section])
        return stream_ref[...] + query_ref[section].astype(F32) * filtered

    def short_section(section, tap_set):
        values = gated(section)
        for index, half in enumerate(halves):
            padded_ref[tap_set, index, ROWS:] = values[:, half]
        hand = None
        if tap_set:

            @pl.when(has_before)
            def _():
                for index, half in enumerate(halves):
                    padded_ref[tap_set, index, :ROWS] = state_ref[modes:, half]

        else:
            hand = hand_over(
                section,
                padded_ref.at[tap_set, :, pl.ds(length, ROWS)],
                padded_ref.at[tap_set, :, pl.ds(0, ROWS)],
            )

            @pl.when(has_after)
            def _():
                hand.start()

            @pl.when(has_before)
            def _():
                hand.wait_recv()

        filtered = []
        for index, half in enumerate(halves):
            taps = short_ref[:, tap_set, half]
            total = values[:, half] * taps[:1]
            for tap in range(1, taps.shape[0]):
                rows = padded_ref[tap_set, index, pl.ds(ROWS - tap, length)]
                total = total + rows * taps[tap : tap + 1]
            filtered.append(total)
        return hand, advance(section, jnp.concatenate(filtered, axis=1))

    def from_spectrum(index, spectrum):
        real, imag = spectrum[:length], spectrum[length:]
        first, cross, last = (spectra_ref[index, place] for place in range(3))
        product = jnp.concatenate(
            [real * first - imag * cross, real * cross + imag * last], axis=0
        )
        return times(back_ref[...], product)

    def medium_section(section):
        hand = hand_over(section, gated_ref, rows_ref)
        gated_ref[...] = gated(section).astype(BF16)

        @pl.when(has_after)
        def _():
            hand.start()

        arrived(query_ref.at[section], query_recv.at[section])

        def finish(spectrum):
            filtered = from_spectrum(0, spectrum)
            stream_ref[...] += query_ref[section].astype(F32) * filtered

        @pl.when(jnp.logical_not(has_before))
        def _():
            finish(times(own_ref[0], gated_ref[...]))

        @pl.when(has_before)
        def _():
            hand.wait_recv()
            both = jnp.concatenate([gated_ref[...], rows_ref[...]], axis=0)
            finish(times(all_ref[...], both))

        return hand

    def long_section(section):
        hand = hand_over(section, leaving_ref, state_ref)
        values = gated(section)
        arrived(query_ref.at[section], query_recv.at[section])

        arrived(key_ref.at[section + 1], key_recv.at[section + 1])
        end = pl.ds(length - ROWS, ROWS)

        def leave():
            for mode in range(modes):
                leaving_ref[mode : mode + 1] = jnp.sum(
                    age_ref[mode] * values, axis=0, keepdims=True
                )

        def send_end():
            states = leaving_ref[:modes]
            rows = values[length - ROWS :]
            filtered = ending_ref[0] * states[:1]
            for mode in range(1, modes):
                filtered = filtered + ending_ref[mode] * states[mode : mode + 1]
            for row in range(ROWS):
                filtered = filtered + within_ref[row] * rows[row : row + 1]
            stream = stream_ref[end] + query_ref[section, end].astype(F32) * filtered
            leaving_ref[modes:] = key_ref[section + 1, end].astype(F32) * stream
            hand.start()

        @pl.when(jnp.logical_not(has_before))
        def _():
            spectrum = times(own_ref[0], values)
            if n_ctx > 1:
                leave()
                send_end()
            filtered = from_spectrum(1, spectrum)
            stream_ref[...] += query_ref[section].astype(F32) * filtered

        @pl.when(has_before)
        def _():
            filtered = from_spectrum(1, times(own_ref[0], values))
            waiting_ref[...] = stream_ref[...] + query_ref[section].astype(F32) * filtered

            if n_ctx > 2:
                pl.when(has_after)(leave)

            hand.wait_recv()
            states = state_ref[:modes]

            if n_ctx > 2:

                @pl.when(has_after)
                def _():
                    leaving_ref[:modes] += decay_ref[1] * states
                    send_end()

            entering = decay_ref[0] * states
            carried = carry_ref[0] * entering[:1]
            for mode in range(1, modes):
                carried = carried + carry_ref[mode] * entering[mode : mode + 1]
            stream_ref[...] = waiting_ref[...] + query_ref[section].astype(F32) * carried

        return hand

    hands = []
    for section in range(sections):
        if section < sections - 1:
            arrived(key_ref.at[section], key_recv.at[section])
        if section == 1:
            hands.append(medium_section(section))
        elif section == 2:
            hands.append(long_section(section))
        else:
            hand, stream = short_section(section, min(section, 1))
            if section:
                out[...] = stream.astype(BF16)
            else:
                hands.append(hand)
                stream_ref[...] = stream

    arrived(sums_ref.at[pl.ds(0, peers)], sum_send)

    @pl.when(jnp.logical_not(led))
    def _():
        arrived(key_ref.at[pl.ds(0, sections - 1)], key_send)

    arrived(query_ref.at[pl.ds(0, sections - 1)], query_send)

    @pl.when(has_after)
    def _():
        for hand in hands:
            hand.wait_send()


def shards(
    inputs,
    query_fields,
    key_fields,
    norm_gain,
    short_taps,
    medium_taps,
    pole_rates,
    pole_residues,
    direct_term,
):
    sections = lax.axis_size("sec")
    n_ctx = lax.axis_size("ctx")
    n_ch = lax.axis_size("ch")
    length, width = inputs.shape
    modes = pole_rates.shape[0]
    shorts, short_span = short_taps.shape[:2]
    tables = waves(length)
    anywhere = pl.BlockSpec(memory_space=pl.ANY)
    dma = pltpu.SemaphoreType.DMA
    return pl.pallas_call(
        functools.partial(kernel, sections, n_ctx, n_ch),
        out_shape=jax.ShapeDtypeStruct((length, width), inputs.dtype),
        in_specs=[anywhere] * 12,
        out_specs=pl.BlockSpec(memory_space=pltpu.VMEM),
        scratch_shapes=[
            pltpu.VMEM((length, width), inputs.dtype),
            pltpu.VMEM((1, width), F32),
            pltpu.VMEM((short_span, shorts, width), F32),
            pltpu.VMEM((medium_taps.shape[0], width), F32),
            pltpu.VMEM((modes, width), F32),
            pltpu.VMEM((modes, width), F32),
            pltpu.VMEM((1, width), F32),
            pltpu.VMEM((sections, length, width), key_fields.dtype),
            pltpu.VMEM((sections, length, width), query_fields.dtype),
            pltpu.VMEM((n_ch * sections, 1, length), F32),
            pltpu.VMEM((2, width // LANES, ROWS + length, LANES), F32),
            pltpu.VMEM((length, width), BF16),
            pltpu.VMEM((length, width), BF16),
            pltpu.VMEM((length, width), F32),
            pltpu.VMEM((length, width), F32),
            pltpu.VMEM((length, width), F32),
            pltpu.VMEM((modes + ROWS, width), F32),
            pltpu.VMEM((modes + ROWS, width), F32),
            pltpu.VMEM((modes, length, width), F32),
            pltpu.VMEM((modes, length, width), F32),
            pltpu.VMEM((2, modes, width), F32),
            pltpu.VMEM((modes, ROWS, width), F32),
            pltpu.VMEM((ROWS, ROWS, width), F32),
            pltpu.VMEM(tables[0].shape, BF16),
            pltpu.VMEM(tables[1].shape, BF16),
            pltpu.VMEM(tables[2].shape, BF16),
            pltpu.VMEM((2, 3, length, width), F32),
            dma((10,)),
            dma,
            dma((sections,)),
            dma,
            dma((sections,)),
            dma,
            dma,
            dma((sections,)),
            dma((sections,)),
            pltpu.SemaphoreType.REGULAR((sections,)),
            pltpu.SemaphoreType.REGULAR,
            pltpu.SemaphoreType.REGULAR,
            pltpu.SemaphoreType.REGULAR,
        ],
        compiler_params=pltpu.CompilerParams(collective_id=0, has_side_effects=True, vmem_limit_bytes=8*2**20),
    )(*[pltpu.with_memory_space_constraint(a, pltpu.HBM) for a in (
        inputs,
        query_fields,
        key_fields,
        norm_gain[None],
        jnp.swapaxes(short_taps, 0, 1),
        medium_taps,
        pole_rates,
        pole_residues,
        direct_term[None],
        *(jnp.asarray(table) for table in tables),
    )])


def solution(mesh):
    in_specs = (
        P("ctx", ("ch", "sec")),
        P("sec", "ctx", "ch"),
        P("sec", "ctx", "ch"),
        P("ch"),
        P(None, None, "ch"),
        P(None, "ch"),
        P(None, "ch"),
        P(None, "ch"),
        P("ch"),
    )
    out_specs = P("ctx", ("ch", "sec"))
    return jax.shard_map(shards, mesh=mesh, in_specs=in_specs, out_specs=out_specs, check_vma=False)
```
